128 devices in a mesh: seq: 64 (over x_lo, y, z, core), fsdp: 2 (over x_hi).
Axes of the slice: x: 4 (x_hi: 2, x_lo: 2; x = x_hi * 2 + x_lo), y: 4, z: 4, core: 2. Of those that a mesh axis runs over, the one named last changes fastest.
Arguments:
- tokens: bfloat16 [32768, 5376], P(('seq', 'fsdp')), may hold values from -6 to 6
- norm_gain: float32 [5376], replicated, may hold values from 0.1 to 1.9
- query_weight: bfloat16 [5376, 2048], P('seq', 'fsdp'), may hold values from -0.078125 to 0.078125
- key_matrix: bfloat16 [5376, 1024], P('seq', 'fsdp'), may hold values from -0.078125 to 0.078125
- value_matrix: bfloat16 [5376, 1024], P('seq', 'fsdp'), may hold values from -0.078125 to 0.078125
- out_weight: bfloat16 [5376, 2048], P('seq', 'fsdp'), may hold values from -0.125 to 0.125
- query_gain: float32 [128], replicated, may hold values from 0.1 to 1.9
- key_gain: float32 [128], replicated, may hold values from 0.1 to 1.9
- post_gain: float32 [5376], replicated, may hold values from 0.1 to 1.9
Outputs:
- layer_out: bfloat16 [32768, 5376], P(('seq', 'fsdp'))
The draws below stay inside these ranges and needn't reach their ends.
All inputs are finite; a program needn't handle non-finite values.
Results may differ from the reference program's by a relative error of at most 0.011.
Values may be sent and summed in bfloat16 or wider, within the bound.
No kernel may reach another device: no remote copies, remote signals or barrier semaphores. Data moves between devices by JAX's collectives and lax.ppermute only.
A program may use at most 192 MiB of HBM per device.

```python
import jax
import jax.numpy as jnp
from jax import lax

MODEL_WIDTH = 5376
HEAD_SIZE = 128
QUERY_HEADS = 16
KEY_VALUE_HEADS = 8
WINDOW_LENGTH = 1024
TOKENS = 32768
N_FSDP = 2


def levels(rng, extent, split, least, high):
    level = 1.0
    for dim, shards_of in split:
        steps = jax.random.uniform(jax.random.fold_in(jax.random.fold_in(rng, 6), dim), (shards_of,), jnp.float32, least / len(split), high / len(split))
        level = level * jnp.repeat(jnp.exp(steps), extent[dim] // shards_of).reshape((-1,) + (1,) * (len(extent) - 1 - dim))
    return level


def bell_draw(stream_key, dims, scale, most, pieces=(), kind=jnp.bfloat16):
    loudness = levels(stream_key, dims, pieces, -0.22, 0.18) if pieces else 1.0
    drawn = jax.random.normal(stream_key, dims, jnp.float32) * scale * loudness
    return jnp.minimum(jnp.maximum(drawn, -most), most).astype(kind)


def setup_inputs(seed: int = 0) -> dict:
    key_of = jax.random.split(jax.random.key(seed), 10)
    return {
        "tokens": bell_draw(key_of[0], (TOKENS, MODEL_WIDTH), 1.0, 6.0, ((0, 128),)),
        "norm_gain": jnp.clip(1.0 + 0.18 * jax.random.normal(key_of[1], (MODEL_WIDTH,), jnp.float32), 0.1, 1.9),
        "query_weight": bell_draw(key_of[2], (MODEL_WIDTH, QUERY_HEADS * HEAD_SIZE), MODEL_WIDTH ** -0.5, 0.078125, ((0, 64), (1, 2))),
        "key_matrix": bell_draw(key_of[3], (MODEL_WIDTH, KEY_VALUE_HEADS * HEAD_SIZE), MODEL_WIDTH ** -0.5, 0.078125, ((0, 64), (1, 2))),
        "value_matrix": bell_draw(key_of[4], (MODEL_WIDTH, KEY_VALUE_HEADS * HEAD_SIZE), MODEL_WIDTH ** -0.5, 0.078125, ((0, 64), (1, 2))),
        "out_weight": bell_draw(key_of[5], (MODEL_WIDTH, QUERY_HEADS * HEAD_SIZE), (QUERY_HEADS * HEAD_SIZE) ** -0.5, 0.125, ((0, 64), (1, 2))),
        "query_gain": jnp.clip(1.0 + 0.18 * jax.random.normal(key_of[6], (HEAD_SIZE,), jnp.float32), 0.1, 1.9),
        "key_gain": jnp.clip(1.0 + 0.18 * jax.random.normal(key_of[7], (HEAD_SIZE,), jnp.float32), 0.1, 1.9),
        "post_gain": jnp.clip(1.0 + 0.18 * jax.random.normal(key_of[8], (MODEL_WIDTH,), jnp.float32), 0.1, 1.9),
    }


epsilon = 1e-06
score_scale = 168.0 ** (-0.5)
rope_base = 10000.0
masked_score = -1e+30

def rms_scaled(values, gain):
    mean_square = lax.optimization_barrier(jnp.mean(values * values, axis=-1, keepdims=True))
    return values * lax.rsqrt(mean_square + epsilon) * gain

def rotary(values, positions):
    half_width = values.shape[-1] // 2
    exponents = jnp.arange(half_width, dtype=jnp.float32) * (2.0 / values.shape[-1])
    frequency = jnp.exp(-exponents * jnp.log(jnp.float32(rope_base)))
    angles = positions.astype(jnp.float32)[:, None] * frequency[None, :]
    cosine = jnp.cos(angles)[:, None, :]
    sine = jnp.sin(angles)[:, None, :]
    first_half = values[..., :half_width]
    second_half = values[..., half_width:]
    return jnp.concatenate([first_half * cosine - second_half * sine, second_half * cosine + first_half * sine], axis=-1)

def head_states(projected, gain, positions):
    shaped = projected.reshape(projected.shape[0], -1, HEAD_SIZE)
    return rotary(rms_scaled(shaped, gain), positions).astype(jnp.bfloat16)

def window_block(query_block, key_block, value_block, query_pos, key_pos):
    scores = jnp.einsum('rkgd,lkd->kgrl', query_block.astype(jnp.float32), key_block.astype(jnp.float32), precision=lax.Precision.HIGHEST) * score_scale
    offset = query_pos[:, None] - key_pos[None, :]
    allowed = (offset >= 0) & (offset < WINDOW_LENGTH) & (key_pos[None, :] >= 0)
    scores = jnp.where(allowed, scores, masked_score)
    highest = lax.optimization_barrier(jnp.max(scores, axis=-1, keepdims=True))
    raised = jnp.exp(scores - highest)
    weights = (raised / lax.optimization_barrier(jnp.sum(raised, axis=-1, keepdims=True))).astype(jnp.bfloat16)
    mixed = jnp.einsum('kgrl,lkd->rkgd', weights.astype(jnp.float32), value_block.astype(jnp.float32), precision=lax.Precision.HIGHEST)
    return mixed.astype(jnp.bfloat16).reshape(query_block.shape[0], -1)

def reference(tokens, norm_gain, query_weight, key_matrix, value_matrix, out_weight, query_gain, key_gain, post_gain):
    row_count = tokens.shape[0]
    query_groups = QUERY_HEADS // KEY_VALUE_HEADS
    normed_input = rms_scaled(tokens.astype(jnp.float32), norm_gain).astype(jnp.bfloat16)
    positions = jnp.arange(row_count, dtype=jnp.int32)
    query_states = head_states(jnp.dot(normed_input, query_weight, preferred_element_type=jnp.float32), query_gain, positions)
    query_states = query_states.reshape(row_count, KEY_VALUE_HEADS, query_groups, HEAD_SIZE)
    keys_all = head_states(jnp.dot(normed_input, key_matrix, preferred_element_type=jnp.float32), key_gain, positions)
    value_states = jnp.dot(normed_input, value_matrix, preferred_element_type=jnp.float32).astype(jnp.bfloat16).reshape(row_count, KEY_VALUE_HEADS, HEAD_SIZE)
    padding_rows = jnp.zeros((WINDOW_LENGTH, KEY_VALUE_HEADS, HEAD_SIZE), jnp.bfloat16)
    padded_keys = jnp.concatenate([padding_rows, keys_all], axis=0)
    padded_values = jnp.concatenate([padding_rows, value_states], axis=0)

    def one_block(block_index):
        begin = (block_index * WINDOW_LENGTH).astype(jnp.int32)
        query_block = lax.dynamic_slice_in_dim(query_states, begin, WINDOW_LENGTH, 0)
        key_block = lax.dynamic_slice_in_dim(padded_keys, begin, 2 * WINDOW_LENGTH, 0)
        value_block = lax.dynamic_slice_in_dim(padded_values, begin, 2 * WINDOW_LENGTH, 0)
        query_pos = begin + jnp.arange(WINDOW_LENGTH, dtype=jnp.int32)
        key_pos = begin - WINDOW_LENGTH + jnp.arange(2 * WINDOW_LENGTH, dtype=jnp.int32)
        return window_block(query_block, key_block, value_block, query_pos, key_pos)
    blocks = lax.map(one_block, jnp.arange(row_count // WINDOW_LENGTH, dtype=jnp.int32))
    attended = blocks.reshape(row_count, QUERY_HEADS * HEAD_SIZE)
    group_width = QUERY_HEADS * HEAD_SIZE // N_FSDP
    projected = jnp.zeros((row_count, out_weight.shape[0]), jnp.float32)
    for group in range(N_FSDP):
        left = attended[:, group * group_width:(group + 1) * group_width]
        right = out_weight[:, group * group_width:(group + 1) * group_width]
        term = lax.dot_general(left, right, (((1,), (1,)), ((), ())), preferred_element_type=jnp.float32)
        projected = projected + term.astype(jnp.bfloat16).astype(jnp.float32)
    return (tokens.astype(jnp.float32) + rms_scaled(projected, post_gain)).astype(jnp.bfloat16)
```

```python
import math

import jax
import jax.numpy as jnp
from jax import lax
from jax.experimental import pallas as pl
from jax.experimental.pallas import tpu as pltpu
from jax.sharding import Mesh, PartitionSpec as P

HEAD = 128
HALF = HEAD // 2
BLOCK = 256
WIDTH = 5376
AXES = ("x_lo", "y", "z", "core", "x_hi")
CHIPS = ("x_lo", "y", "z")
GATHER = ("x_hi", "x_lo", "y", "z")
epsilon = 1e-06
query_scale = 168.0 ** (-0.5) * math.log2(math.e)
rope_base = 10000.0
BF = jnp.bfloat16
F32 = jnp.float32
MIB = 1 << 20


def cost(flops, size, exps=0):
    return pl.CostEstimate(flops=int(flops), bytes_accessed=int(size), transcendentals=int(exps))


def params(mib):
    return pltpu.CompilerParams(vmem_limit_bytes=mib * MIB)


def turned(raw, gain, cosine, sine, scale):
    mean_square = jnp.mean(raw * raw, axis=-1, keepdims=True)
    unit = raw * (lax.rsqrt(mean_square + epsilon) * scale) * gain
    return unit * cosine + pltpu.roll(unit, HALF, axis=1) * sine


def key_value_kernel(x_ref, w_ref, gain_ref, cos_ref, sin_ref, out_ref):
    raw = jnp.dot(x_ref[...], w_ref[...], preferred_element_type=F32)

    @pl.when(pl.program_id(0) < 2)
    def _():
        for h in range(2):
            at = slice(h * HEAD, (h + 1) * HEAD)
            key = turned(raw[:, at], gain_ref[...], cos_ref[...], sin_ref[...], 1.0)
            out_ref[:, at] = key.astype(BF)

    @pl.when(pl.program_id(0) >= 2)
    def _():
        out_ref[...] = raw.astype(BF)


def query_kernel(x_ref, w_ref, gain_ref, cos_ref, sin_ref, out_ref):
    raw = jnp.dot(x_ref[...], w_ref[...], preferred_element_type=F32)
    for h in range(2):
        at = slice(h * HEAD, (h + 1) * HEAD)
        query = turned(raw[:, at], gain_ref[...], cos_ref[...], sin_ref[...], query_scale)
        out_ref[:, at] = query.astype(BF)


def projection(kernel, x, weights, gain, cosine, sine, where):
    rows = x.shape[0]
    whole = pl.BlockSpec(memory_space=pltpu.VMEM)
    return pl.pallas_call(
        kernel,
        out_shape=jax.ShapeDtypeStruct((rows, 1024), BF),
        grid=(4,),
        in_specs=[whole, pl.BlockSpec((WIDTH, 256), where), whole, whole, whole],
        out_specs=pl.BlockSpec((rows, 256), lambda t: (0, t)),
        compiler_params=params(48),
        cost_estimate=cost(2 * rows * WIDTH * 1024, 2 * WIDTH * 1536),
    )(x, weights, gain, cosine, sine)


def attention_kernel(flag_ref, q_ref, ok, ov, zk, zv, ak, av, bk, bv, ck, cv, out_ref):
    core = flag_ref[2]
    lane = lax.broadcasted_iota(jnp.int32, (BLOCK, HEAD), 1)
    ones = jnp.where(lane == 0, 1.0, 0.0).astype(F32)
    early = (ones * flag_ref[0].astype(F32)).astype(BF)
    before = (ones * flag_ref[1].astype(F32)).astype(BF)
    ones = ones.astype(BF)
    first, second = slice(0, BLOCK), slice(BLOCK, 2 * BLOCK)
    own0 = (ok.at[first], ov.at[first], ones)
    own1 = (ok.at[second], ov.at[second], ones)
    far = (zk.at[first], zv.at[first], early)
    mid = (zk.at[second], zv.at[second], early)
    prior = (ak, av, before)
    gap = (bk, bv, early)
    link = (ck, cv, ones)
    row = lax.rem(lax.broadcasted_iota(jnp.int32, (2 * BLOCK, BLOCK), 0), BLOCK)
    col = lax.broadcasted_iota(jnp.int32, (2 * BLOCK, BLOCK), 1)
    for part, keys in enumerate(((far, gap, mid, prior, own0), (mid, prior, own0, link, own1))):
        at = slice(part * BLOCK, (part + 1) * BLOCK)
        query = jnp.concatenate([q_ref[at, :HEAD], q_ref[at, HEAD:]], axis=0)
        total = jnp.zeros((2 * BLOCK, 2 * HEAD), F32)
        for n, (k, v, tail) in enumerate(keys):
            score = lax.dot_general(
                query, k[...], (((1,), (1,)), ((), ())), preferred_element_type=F32
            )
            raised = jnp.exp2(score)
            if n == 0:
                raised = jnp.where(col > row, raised, 0.0)
            if n == 4:
                raised = jnp.where(col <= row, raised, 0.0)
            value = jnp.concatenate([v[...], tail], axis=1)
            total += jnp.dot(raised.astype(BF), value, preferred_element_type=F32)
        mixed = (total[:, :HEAD] / total[:, HEAD : HEAD + 1]).astype(BF)
        to = pl.multiple_of(lax.rem(part + core, 2) * BLOCK, BLOCK)
        out_ref[pl.ds(to, BLOCK), :HEAD] = mixed[:BLOCK]
        out_ref[pl.ds(to, BLOCK), HEAD:] = mixed[BLOCK:]


def attention(flags, queries, own, behind, prior, gap, link):
    def pair(rows):
        return [
            pl.BlockSpec((rows, HEAD), lambda j: (0, j)),
            pl.BlockSpec((rows, HEAD), lambda j: (0, j + 4)),
        ]

    wide = pl.BlockSpec((2 * BLOCK, 2 * HEAD), lambda j: (0, j))
    return pl.pallas_call(
        attention_kernel,
        out_shape=jax.ShapeDtypeStruct((2 * BLOCK, 1024), BF),
        grid=(4,),
        in_specs=[pl.BlockSpec(memory_space=pltpu.SMEM), wide]
        + pair(512) + pair(512) + pair(256) + pair(256) + pair(256),
        out_specs=wide,
        compiler_params=params(32),
        cost_estimate=cost(8 * 512 * 1280 * 512, 6 * MIB, 8 * 512 * 1280),
    )(flags, queries, own, own, behind, behind, prior, prior, gap, gap, link, link)


def out_kernel(att_ref, low_ref, high_ref, own_ref, other_ref):
    dims = (((1,), (1,)), ((), ()))
    got = lax.dot_general(att_ref[:, :512], low_ref[...], dims, preferred_element_type=F32)
    got += lax.dot_general(att_ref[:, 512:], high_ref[...], dims, preferred_element_type=F32)
    own_ref[...] = got[:BLOCK]
    other_ref[...] = got[BLOCK:].astype(BF)


def out_projection(attended, weights, half):
    tile, steps = 896, 3
    first = half * steps
    return pl.pallas_call(
        out_kernel,
        out_shape=(
            jax.ShapeDtypeStruct((BLOCK, WIDTH // 2), F32),
            jax.ShapeDtypeStruct((BLOCK, WIDTH // 2), BF),
        ),
        grid=(steps,),
        in_specs=[
            pl.BlockSpec(memory_space=pltpu.VMEM),
            pl.BlockSpec((tile, 512), lambda i: (first + i, 0)),
            pl.BlockSpec((tile, 512), lambda i: (first + i + 2 * steps, 0)),
        ],
        out_specs=(
            pl.BlockSpec((BLOCK, tile), lambda i: (0, i)),
            pl.BlockSpec((BLOCK, tile), lambda i: (0, i)),
        ),
        compiler_params=params(32),
        cost_estimate=cost(2 * 512 * 1024 * WIDTH // 2, 10 * MIB),
    )(attended, weights, weights)


def end_kernel(tok_ref, own0, own1, got0, got1, gain_ref, out_ref):
    middle = WIDTH // 2
    left = own0[...] + got0[...].astype(F32)
    right = own1[...] + got1[...].astype(F32)
    square = jnp.sum(left * left, axis=-1, keepdims=True)
    square += jnp.sum(right * right, axis=-1, keepdims=True)
    factor = lax.rsqrt(square * (1.0 / WIDTH) + epsilon)
    for n, part in enumerate((left, right)):
        at = slice(n * middle, (n + 1) * middle)
        scaled = part * factor * gain_ref[:, at]
        out_ref[:, at] = (tok_ref[:, at].astype(F32) + scaled).astype(BF)


def ending(tokens, own0, own1, got0, got1, gain):
    rows = 64
    half = pl.BlockSpec((rows, WIDTH // 2), lambda i: (i, 0))
    wide = pl.BlockSpec((rows, WIDTH), lambda i: (i, 0))
    return pl.pallas_call(
        end_kernel,
        out_shape=jax.ShapeDtypeStruct((BLOCK, WIDTH), BF),
        grid=(BLOCK // rows,),
        in_specs=[wide, half, half, half, half, pl.BlockSpec((1, WIDTH), lambda i: (0, 0))],
        out_specs=wide,
        compiler_params=params(32),
        cost_estimate=cost(10 * BLOCK * WIDTH, 14 * MIB),
    )(tokens, own0, own1, got0, got1, gain)


def rotations(positions):
    exponents = jnp.arange(HALF, dtype=F32) * (2.0 / HEAD)
    frequency = jnp.exp(-exponents * jnp.log(jnp.float32(rope_base)))
    angles = positions.astype(F32)[:, None] * frequency[None, :]
    cosine, sine = jnp.cos(angles), jnp.sin(angles)
    return (
        jnp.concatenate([cosine, cosine], axis=1),
        jnp.concatenate([-sine, sine], axis=1),
    )


def quarter_rows(pieces):
    rows = pieces[0].shape[0]
    sides = [
        jnp.concatenate([p[:, s * p.shape[1] // 2 : (s + 1) * p.shape[1] // 2] for p in pieces], 1)
        for s in range(2)
    ]
    swapped = lax.all_to_all(jnp.stack(sides), "core", 0, 0, tiled=True)
    return swapped.reshape(2 * rows, -1)


def on_device(
    tokens,
    norm_gain,
    query_weight,
    key_matrix,
    value_matrix,
    out_weight,
    query_gain,
    key_gain,
    post_gain,
):
    core = lax.axis_index("core")
    side = lax.axis_index("x_hi")
    chip = lax.axis_index(CHIPS)
    qkv = lax.all_gather(
        quarter_rows([query_weight, key_matrix, value_matrix]), GATHER, axis=0, tiled=True
    )
    out_rows = quarter_rows([out_weight])

    plain = tokens.astype(F32)
    mean_square = jnp.mean(plain * plain, axis=-1, keepdims=True)
    normed = (plain * lax.rsqrt(mean_square + epsilon) * norm_gain).astype(BF)
    other = lax.ppermute(normed, "core", [(0, 1), (1, 0)])
    x = jnp.concatenate(
        [jnp.where(core == 0, normed, other), jnp.where(core == 0, other, normed)], axis=0
    )
    row = jnp.arange(2 * BLOCK, dtype=jnp.int32)
    positions = (4 * chip + side) * BLOCK + row + (row // BLOCK) * BLOCK
    cosine, sine = rotations(positions)

    qkv, out_rows = lax.optimization_barrier((qkv, out_rows))
    out_full = lax.all_gather(out_rows, GATHER, axis=0, tiled=True)

    own = projection(
        key_value_kernel, x, qkv, key_gain.reshape(1, HEAD), cosine, sine,
        lambda t: (lax.rem(t, 2), 2 + t // 2),
    )
    first, second = own[:BLOCK], own[BLOCK:]
    mine = jnp.where(side == 0, first, second)
    swap = jnp.where(side == 0, second, first)
    line = CHIPS + ("x_hi",)
    chips = 32
    prior = lax.ppermute(mine, line, [(i, i + 1) for i in range(2 * chips - 1)])
    gap = lax.ppermute(
        swap, line,
        [(2 * i + 1, 2 * i + 2) for i in range(chips - 1)]
        + [(2 * i, 2 * i + 3) for i in range(chips - 1)],
    )
    link = lax.ppermute(swap, "x_hi", [(0, 1), (1, 0)])
    behind = lax.ppermute(own, CHIPS, [(i, i + 1) for i in range(chips - 1)])
    queries = projection(
        query_kernel, x, qkv, query_gain.reshape(1, HEAD), cosine, sine,
        lambda t: (t // 2, lax.rem(t, 2)),
    )
    later = (chip > 0).astype(jnp.int32)
    flags = jnp.stack([later, jnp.maximum(later, side), core]).astype(jnp.int32)
    attended = attention(flags, queries, own, behind, prior, gap, link)
    own0, send0 = out_projection(attended, out_full, 0)
    got0 = lax.ppermute(send0, "core", [(0, 1), (1, 0)])
    own1, send1 = out_projection(attended, out_full, 1)
    got1 = lax.ppermute(send1, "core", [(0, 1), (1, 0)])
    return ending(tokens, own0, own1, got0, got1, post_gain.reshape(1, WIDTH))


def solution(mesh):
    spread = Mesh(mesh.devices.reshape(2, 4, 4, 2, 2), AXES)
    whole = P(AXES, None)
    rows = P(AXES[:4], "x_hi")
    return jax.shard_map(
        on_device,
        mesh=spread,
        in_specs=(whole, P(), rows, rows, rows, rows, P(), P(), P()),
        out_specs=whole,
        check_vma=False,
    )
```

```python
import math

import jax
import jax.numpy as jnp
from jax import lax
from jax.experimental import pallas as pl
from jax.experimental.pallas import tpu as pltpu
from jax.sharding import Mesh, PartitionSpec as P

HEAD = 128
HALF = HEAD // 2
BLOCK = 256
WIDTH = 5376
AXES = ("x_lo", "y", "z", "core", "x_hi")
CHIPS = ("x_lo", "y", "z")
GATHER = ("x_hi", "x_lo", "y", "z")
epsilon = 1e-06
query_scale = 168.0 ** (-0.5) * math.log2(math.e)
rope_base = 10000.0
BF = jnp.bfloat16
F32 = jnp.float32
MIB = 1 << 20


def cost(flops, size, exps=0):
    return pl.CostEstimate(flops=int(flops), bytes_accessed=int(size), transcendentals=int(exps))


def params(mib):
    return pltpu.CompilerParams(vmem_limit_bytes=mib * MIB)


def turned(raw, gain, cosine, sine, scale):
    mean_square = jnp.mean(raw * raw, axis=-1, keepdims=True)
    unit = raw * (lax.rsqrt(mean_square + epsilon) * scale) * gain
    return unit * cosine + pltpu.roll(unit, HALF, axis=1) * sine


def key_value_kernel(x_ref, w_ref, gain_ref, cos_ref, sin_ref, out_ref):
    raw = jnp.dot(x_ref[...], w_ref[...], preferred_element_type=F32)

    @pl.when(pl.program_id(0) < 2)
    def _():
        for h in range(2):
            at = slice(h * HEAD, (h + 1) * HEAD)
            key = turned(raw[:, at], gain_ref[...], cos_ref[...], sin_ref[...], 1.0)
            out_ref[:, at] = key.astype(BF)

    @pl.when(pl.program_id(0) >= 2)
    def _():
        out_ref[...] = raw.astype(BF)


def query_kernel(x_ref, w_ref, gain_ref, cos_ref, sin_ref, out_ref):
    raw = jnp.dot(x_ref[...], w_ref[...], preferred_element_type=F32)
    for h in range(2):
        at = slice(h * HEAD, (h + 1) * HEAD)
        query = turned(raw[:, at], gain_ref[...], cos_ref[...], sin_ref[...], query_scale)
        out_ref[:, at] = query.astype(BF)


def projection(kernel, x, weights, gain, cosine, sine, where):
    rows = x.shape[0]
    whole = pl.BlockSpec(memory_space=pltpu.VMEM)
    return pl.pallas_call(
        kernel,
        out_shape=jax.ShapeDtypeStruct((rows, 1024), BF),
        grid=(4,),
        in_specs=[whole, pl.BlockSpec((WIDTH, 256), where), whole, whole, whole],
        out_specs=pl.BlockSpec((rows, 256), lambda t: (0, t)),
        compiler_params=params(48),
        cost_estimate=cost(2 * rows * WIDTH * 1024, 2 * WIDTH * 1536),
    )(x, weights, gain, cosine, sine)


def attention_kernel(flag_ref, q_ref, ok, ov, zk, zv, ak, av, bk, bv, ck, cv, out_ref):
    core = flag_ref[2]
    lane = lax.broadcasted_iota(jnp.int32, (BLOCK, HEAD), 1)
    ones = jnp.where(lane == 0, 1.0, 0.0).astype(F32)
    early = (ones * flag_ref[0].astype(F32)).astype(BF)
    before = (ones * flag_ref[1].astype(F32)).astype(BF)
    ones = ones.astype(BF)
    first, second = slice(0, BLOCK), slice(BLOCK, 2 * BLOCK)
    own0 = (ok.at[first], ov.at[first], ones)
    own1 = (ok.at[second], ov.at[second], ones)
    far = (zk.at[first], zv.at[first], early)
    mid = (zk.at[second], zv.at[second], early)
    prior = (ak, av, before)
    gap = (bk, bv, early)
    link = (ck, cv, ones)
    row = lax.rem(lax.broadcasted_iota(jnp.int32, (2 * BLOCK, BLOCK), 0), BLOCK)
    col = lax.broadcasted_iota(jnp.int32, (2 * BLOCK, BLOCK), 1)
    for part, keys in enumerate(((far, gap, mid, prior, own0), (mid, prior, own0, link, own1))):
        at = slice(part * BLOCK, (part + 1) * BLOCK)
        query = jnp.concatenate([q_ref[at, :HEAD], q_ref[at, HEAD:]], axis=0)
        total = jnp.zeros((2 * BLOCK, 2 * HEAD), F32)
        for n, (k, v, tail) in enumerate(keys):
            score = lax.dot_general(
                query, k[...], (((1,), (1,)), ((), ())), preferred_element_type=F32
            )
            raised = jnp.exp2(score)
            if n == 0:
                raised = jnp.where(col > row, raised, 0.0)
            if n == 4:
                raised = jnp.where(col <= row, raised, 0.0)
            value = jnp.concatenate([v[...], tail], axis=1)
            total += jnp.dot(raised.astype(BF), value, preferred_element_type=F32)
        mixed = (total[:, :HEAD] / total[:, HEAD : HEAD + 1]).astype(BF)
        to = pl.multiple_of(lax.rem(part + core, 2) * BLOCK, BLOCK)
        out_ref[pl.ds(to, BLOCK), :HEAD] = mixed[:BLOCK]
        out_ref[pl.ds(to, BLOCK), HEAD:] = mixed[BLOCK:]


def attention(flags, queries, own, behind, prior, gap, link):
    def pair(rows):
        return [
            pl.BlockSpec((rows, HEAD), lambda j: (0, j)),
            pl.BlockSpec((rows, HEAD), lambda j: (0, j + 4)),
        ]

    wide = pl.BlockSpec((2 * BLOCK, 2 * HEAD), lambda j: (0, j))
    return pl.pallas_call(
        attention_kernel,
        out_shape=jax.ShapeDtypeStruct((2 * BLOCK, 1024), BF),
        grid=(4,),
        in_specs=[pl.BlockSpec(memory_space=pltpu.SMEM), wide]
        + pair(512) + pair(512) + pair(256) + pair(256) + pair(256),
        out_specs=wide,
        compiler_params=params(32),
        cost_estimate=cost(8 * 512 * 1280 * 512, 6 * MIB, 8 * 512 * 1280),
    )(flags, queries, own, own, behind, behind, prior, prior, gap, gap, link, link)


def out_kernel(att_ref, low_ref, high_ref, own_ref, other_ref):
    dims = (((1,), (1,)), ((), ()))
    got = lax.dot_general(att_ref[:, :512], low_ref[...], dims, preferred_element_type=F32)
    got += lax.dot_general(att_ref[:, 512:], high_ref[...], dims, preferred_element_type=F32)
    own_ref[...] = got[:BLOCK]
    other_ref[...] = got[BLOCK:].astype(BF)


def out_projection(attended, weights, half):
    tile, steps = 896, 3
    first = half * steps
    return pl.pallas_call(
        out_kernel,
        out_shape=(
            jax.ShapeDtypeStruct((BLOCK, WIDTH // 2), F32),
            jax.ShapeDtypeStruct((BLOCK, WIDTH // 2), BF),
        ),
        grid=(steps,),
        in_specs=[
            pl.BlockSpec(memory_space=pltpu.VMEM),
            pl.BlockSpec((tile, 512), lambda i: (first + i, 2)),
            pl.BlockSpec((tile, 512), lambda i: (first + i + 2 * steps, 2)),
        ],
        out_specs=(
            pl.BlockSpec((BLOCK, tile), lambda i: (0, i)),
            pl.BlockSpec((BLOCK, tile), lambda i: (0, i)),
        ),
        compiler_params=params(32),
        cost_estimate=cost(2 * 512 * 1024 * WIDTH // 2, 10 * MIB),
    )(attended, weights, weights)


def end_kernel(tok_ref, own0, own1, got0, got1, gain_ref, out_ref):
    middle = WIDTH // 2
    left = own0[...] + got0[...].astype(F32)
    right = own1[...] + got1[...].astype(F32)
    square = jnp.sum(left * left, axis=-1, keepdims=True)
    square += jnp.sum(right * right, axis=-1, keepdims=True)
    factor = lax.rsqrt(square * (1.0 / WIDTH) + epsilon)
    for n, part in enumerate((left, right)):
        at = slice(n * middle, (n + 1) * middle)
        scaled = part * factor * gain_ref[:, at]
        out_ref[:, at] = (tok_ref[:, at].astype(F32) + scaled).astype(BF)


def ending(tokens, own0, own1, got0, got1, gain):
    rows = 64
    half = pl.BlockSpec((rows, WIDTH // 2), lambda i: (i, 0))
    wide = pl.BlockSpec((rows, WIDTH), lambda i: (i, 0))
    return pl.pallas_call(
        end_kernel,
        out_shape=jax.ShapeDtypeStruct((BLOCK, WIDTH), BF),
        grid=(BLOCK // rows,),
        in_specs=[wide, half, half, half, half, pl.BlockSpec((1, WIDTH), lambda i: (0, 0))],
        out_specs=wide,
        compiler_params=params(32),
        cost_estimate=cost(10 * BLOCK * WIDTH, 14 * MIB),
    )(tokens, own0, own1, got0, got1, gain)


def rotations(positions):
    exponents = jnp.arange(HALF, dtype=F32) * (2.0 / HEAD)
    frequency = jnp.exp(-exponents * jnp.log(jnp.float32(rope_base)))
    angles = positions.astype(F32)[:, None] * frequency[None, :]
    cosine, sine = jnp.cos(angles), jnp.sin(angles)
    return (
        jnp.concatenate([cosine, cosine], axis=1),
        jnp.concatenate([-sine, sine], axis=1),
    )


def quarter_rows(pieces):
    rows = pieces[0].shape[0]
    sides = [
        jnp.concatenate([p[:, s * p.shape[1] // 2 : (s + 1) * p.shape[1] // 2] for p in pieces], 1)
        for s in range(2)
    ]
    swapped = lax.all_to_all(jnp.stack(sides), "core", 0, 0, tiled=True)
    return swapped.reshape(2 * rows, -1)


def on_device(
    tokens,
    norm_gain,
    query_weight,
    key_matrix,
    value_matrix,
    out_weight,
    query_gain,
    key_gain,
    post_gain,
):
    core = lax.axis_index("core")
    side = lax.axis_index("x_hi")
    chip = lax.axis_index(CHIPS)
    full = lax.all_gather(
        quarter_rows([query_weight, key_matrix, value_matrix, out_weight]),
        GATHER,
        axis=0,
        tiled=True,
    )

    plain = tokens.astype(F32)
    mean_square = jnp.mean(plain * plain, axis=-1, keepdims=True)
    normed = (plain * lax.rsqrt(mean_square + epsilon) * norm_gain).astype(BF)
    other = lax.ppermute(normed, "core", [(0, 1), (1, 0)])
    x = jnp.concatenate(
        [jnp.where(core == 0, normed, other), jnp.where(core == 0, other, normed)], axis=0
    )
    row = jnp.arange(2 * BLOCK, dtype=jnp.int32)
    positions = (4 * chip + side) * BLOCK + row + (row // BLOCK) * BLOCK
    cosine, sine = rotations(positions)

    full, x, cosine, sine = lax.optimization_barrier((full, x, cosine, sine))

    own = projection(
        key_value_kernel, x, full, key_gain.reshape(1, HEAD), cosine, sine,
        lambda t: (lax.rem(t, 2), 2 + t // 2),
    )
    first, second = own[:BLOCK], own[BLOCK:]
    mine = jnp.where(side == 0, first, second)
    swap = jnp.where(side == 0, second, first)
    line = CHIPS + ("x_hi",)
    chips = 32
    prior = lax.ppermute(mine, line, [(i, i + 1) for i in range(2 * chips - 1)])
    gap = lax.ppermute(
        swap, line,
        [(2 * i + 1, 2 * i + 2) for i in range(chips - 1)]
        + [(2 * i, 2 * i + 3) for i in range(chips - 1)],
    )
    link = lax.ppermute(swap, "x_hi", [(0, 1), (1, 0)])
    behind = lax.ppermute(own, CHIPS, [(i, i + 1) for i in range(chips - 1)])
    queries = projection(
        query_kernel, x, full, query_gain.reshape(1, HEAD), cosine, sine,
        lambda t: (t // 2, lax.rem(t, 2)),
    )
    later = (chip > 0).astype(jnp.int32)
    flags = jnp.stack([later, jnp.maximum(later, side), core]).astype(jnp.int32)
    attended = attention(flags, queries, own, behind, prior, gap, link)
    own0, send0 = out_projection(attended, full, 0)
    got0 = lax.ppermute(send0, "core", [(0, 1), (1, 0)])
    own1, send1 = out_projection(attended, full, 1)
    got1 = lax.ppermute(send1, "core", [(0, 1), (1, 0)])
    return ending(tokens, own0, own1, got0, got1, post_gain.reshape(1, WIDTH))


def solution(mesh):
    spread = Mesh(mesh.devices.reshape(2, 4, 4, 2, 2), AXES)
    whole = P(AXES, None)
    rows = P(AXES[:4], "x_hi")
    return jax.shard_map(
        on_device,
        mesh=spread,
        in_specs=(whole, P(), rows, rows, rows, rows, P(), P(), P()),
        out_specs=whole,
        check_vma=False,
    )
```

```python
import math

import jax
import jax.numpy as jnp
from jax import lax
from jax.experimental import pallas as pl
from jax.experimental.pallas import tpu as pltpu
from jax.sharding import Mesh, PartitionSpec as P

HEAD = 128
HALF = HEAD // 2
BLOCK = 256
WIDTH = 5376
AXES = ("x_lo", "y", "z", "core", "x_hi")
CHIPS = ("x_lo", "y", "z")
GATHER = ("x_hi", "x_lo", "y", "z")
epsilon = 1e-06
query_scale = 168.0 ** (-0.5) * math.log2(math.e)
rope_base = 10000.0
BF = jnp.bfloat16
F32 = jnp.float32
MIB = 1 << 20


def cost(flops, size, exps=0):
    return pl.CostEstimate(flops=int(flops), bytes_accessed=int(size), transcendentals=int(exps))


def params(mib):
    return pltpu.CompilerParams(vmem_limit_bytes=mib * MIB)


def turned(raw, gain, cosine, sine, scale):
    mean_square = jnp.mean(raw * raw, axis=-1, keepdims=True)
    unit = raw * (lax.rsqrt(mean_square + epsilon) * scale) * gain
    return unit * cosine + pltpu.roll(unit, HALF, axis=1) * sine


def key_value_kernel(slot_ref, x_ref, *refs):
    unit_refs, (gain_ref, cos_ref, sin_ref, out_ref) = refs[:8], refs[8:]
    weights = jnp.concatenate([ref[0] for ref in unit_refs], axis=0)
    raw = jnp.dot(x_ref[...], weights, preferred_element_type=F32)

    @pl.when(pl.program_id(0) < 2)
    def _():
        for h in range(2):
            at = slice(h * HEAD, (h + 1) * HEAD)
            key = turned(raw[:, at], gain_ref[...], cos_ref[...], sin_ref[...], 1.0)
            out_ref[:, at] = key.astype(BF)

    @pl.when(pl.program_id(0) >= 2)
    def _():
        out_ref[...] = raw.astype(BF)


def query_kernel(x_ref, w_ref, gain_ref, cos_ref, sin_ref, out_ref):
    raw = jnp.dot(x_ref[...], w_ref[...], preferred_element_type=F32)
    for h in range(2):
        at = slice(h * HEAD, (h + 1) * HEAD)
        query = turned(raw[:, at], gain_ref[...], cos_ref[...], sin_ref[...], query_scale)
        out_ref[:, at] = query.astype(BF)


def key_values(slots, x, units, gain, cosine, sine):
    rows = x.shape[0]
    whole = pl.BlockSpec(memory_space=pltpu.VMEM)

    def unit(n):
        return pl.BlockSpec(
            (1, units.shape[1], 256), lambda t, slot: (slot[lax.rem(t, 2) * 8 + n], 0, t // 2)
        )

    return pl.pallas_call(
        key_value_kernel,
        out_shape=jax.ShapeDtypeStruct((rows, 1024), BF),
        grid_spec=pltpu.PrefetchScalarGridSpec(
            num_scalar_prefetch=1,
            grid=(4,),
            in_specs=[whole] + [unit(n) for n in range(8)] + [whole, whole, whole],
            out_specs=pl.BlockSpec((rows, 256), lambda t, slot: (0, t)),
        ),
        compiler_params=params(48),
        cost_estimate=cost(2 * rows * WIDTH * 1024, 2 * WIDTH * 1536),
    )(slots, x, *([units] * 8), gain, cosine, sine)


def projection(kernel, x, weights, gain, cosine, sine, where):
    rows = x.shape[0]
    whole = pl.BlockSpec(memory_space=pltpu.VMEM)
    return pl.pallas_call(
        kernel,
        out_shape=jax.ShapeDtypeStruct((rows, 1024), BF),
        grid=(4,),
        in_specs=[whole, pl.BlockSpec((WIDTH, 256), where), whole, whole, whole],
        out_specs=pl.BlockSpec((rows, 256), lambda t: (0, t)),
        compiler_params=params(48),
        cost_estimate=cost(2 * rows * WIDTH * 1024, 2 * WIDTH * 1536),
    )(x, weights, gain, cosine, sine)


def attention_kernel(flag_ref, q_ref, ok, ov, zk, zv, ak, av, bk, bv, ck, cv, out_ref):
    core = flag_ref[2]
    lane = lax.broadcasted_iota(jnp.int32, (BLOCK, HEAD), 1)
    ones = jnp.where(lane == 0, 1.0, 0.0).astype(F32)
    early = (ones * flag_ref[0].astype(F32)).astype(BF)
    before = (ones * flag_ref[1].astype(F32)).astype(BF)
    ones = ones.astype(BF)
    first, second = slice(0, BLOCK), slice(BLOCK, 2 * BLOCK)
    own0 = (ok.at[first], ov.at[first], ones)
    own1 = (ok.at[second], ov.at[second], ones)
    far = (zk.at[first], zv.at[first], early)
    mid = (zk.at[second], zv.at[second], early)
    prior = (ak, av, before)
    gap = (bk, bv, early)
    link = (ck, cv, ones)
    row = lax.rem(lax.broadcasted_iota(jnp.int32, (2 * BLOCK, BLOCK), 0), BLOCK)
    col = lax.broadcasted_iota(jnp.int32, (2 * BLOCK, BLOCK), 1)
    for part, keys in enumerate(((far, gap, mid, prior, own0), (mid, prior, own0, link, own1))):
        at = slice(part * BLOCK, (part + 1) * BLOCK)
        query = jnp.concatenate([q_ref[at, :HEAD], q_ref[at, HEAD:]], axis=0)
        total = jnp.zeros((2 * BLOCK, 2 * HEAD), F32)
        for n, (k, v, tail) in enumerate(keys):
            score = lax.dot_general(
                query, k[...], (((1,), (1,)), ((), ())), preferred_element_type=F32
            )
            raised = jnp.exp2(score)
            if n == 0:
                raised = jnp.where(col > row, raised, 0.0)
            if n == 4:
                raised = jnp.where(col <= row, raised, 0.0)
            value = jnp.concatenate([v[...], tail], axis=1)
            total += jnp.dot(raised.astype(BF), value, preferred_element_type=F32)
        mixed = (total[:, :HEAD] / total[:, HEAD : HEAD + 1]).astype(BF)
        to = pl.multiple_of(lax.rem(part + core, 2) * BLOCK, BLOCK)
        out_ref[pl.ds(to, BLOCK), :HEAD] = mixed[:BLOCK]
        out_ref[pl.ds(to, BLOCK), HEAD:] = mixed[BLOCK:]


def attention(flags, queries, own, behind, prior, gap, link):
    def pair(rows):
        return [
            pl.BlockSpec((rows, HEAD), lambda j: (0, j)),
            pl.BlockSpec((rows, HEAD), lambda j: (0, j + 4)),
        ]

    wide = pl.BlockSpec((2 * BLOCK, 2 * HEAD), lambda j: (0, j))
    return pl.pallas_call(
        attention_kernel,
        out_shape=jax.ShapeDtypeStruct((2 * BLOCK, 1024), BF),
        grid=(4,),
        in_specs=[pl.BlockSpec(memory_space=pltpu.SMEM), wide]
        + pair(512) + pair(512) + pair(256) + pair(256) + pair(256),
        out_specs=wide,
        compiler_params=params(32),
        cost_estimate=cost(8 * 512 * 1280 * 512, 6 * MIB, 8 * 512 * 1280),
    )(flags, queries, own, own, behind, behind, prior, prior, gap, gap, link, link)


def out_kernel(att_ref, low_ref, high_ref, own_ref, other_ref):
    dims = (((1,), (1,)), ((), ()))
    got = lax.dot_general(att_ref[:, :512], low_ref[...], dims, preferred_element_type=F32)
    got += lax.dot_general(att_ref[:, 512:], high_ref[...], dims, preferred_element_type=F32)
    own_ref[...] = got[:BLOCK]
    other_ref[...] = got[BLOCK:].astype(BF)


def out_projection(attended, weights, half):
    tile, steps = 896, 3
    first = half * steps
    return pl.pallas_call(
        out_kernel,
        out_shape=(
            jax.ShapeDtypeStruct((BLOCK, WIDTH // 2), F32),
            jax.ShapeDtypeStruct((BLOCK, WIDTH // 2), BF),
        ),
        grid=(steps,),
        in_specs=[
            pl.BlockSpec(memory_space=pltpu.VMEM),
            pl.BlockSpec((tile, 512), lambda i: (first + i, 1)),
            pl.BlockSpec((tile, 512), lambda i: (first + i + 2 * steps, 1)),
        ],
        out_specs=(
            pl.BlockSpec((BLOCK, tile), lambda i: (0, i)),
            pl.BlockSpec((BLOCK, tile), lambda i: (0, i)),
        ),
        compiler_params=params(32),
        cost_estimate=cost(2 * 512 * 1024 * WIDTH // 2, 10 * MIB),
    )(attended, weights, weights)


def end_kernel(tok_ref, own0, own1, got0, got1, gain_ref, out_ref):
    middle = WIDTH // 2
    left = own0[...] + got0[...].astype(F32)
    right = own1[...] + got1[...].astype(F32)
    square = jnp.sum(left * left, axis=-1, keepdims=True)
    square += jnp.sum(right * right, axis=-1, keepdims=True)
    factor = lax.rsqrt(square * (1.0 / WIDTH) + epsilon)
    for n, part in enumerate((left, right)):
        at = slice(n * middle, (n + 1) * middle)
        scaled = part * factor * gain_ref[:, at]
        out_ref[:, at] = (tok_ref[:, at].astype(F32) + scaled).astype(BF)


def ending(tokens, own0, own1, got0, got1, gain):
    rows = 64
    half = pl.BlockSpec((rows, WIDTH // 2), lambda i: (i, 0))
    wide = pl.BlockSpec((rows, WIDTH), lambda i: (i, 0))
    return pl.pallas_call(
        end_kernel,
        out_shape=jax.ShapeDtypeStruct((BLOCK, WIDTH), BF),
        grid=(BLOCK // rows,),
        in_specs=[wide, half, half, half, half, pl.BlockSpec((1, WIDTH), lambda i: (0, 0))],
        out_specs=wide,
        compiler_params=params(32),
        cost_estimate=cost(10 * BLOCK * WIDTH, 14 * MIB),
    )(tokens, own0, own1, got0, got1, gain)


def rotations(positions):
    exponents = jnp.arange(HALF, dtype=F32) * (2.0 / HEAD)
    frequency = jnp.exp(-exponents * jnp.log(jnp.float32(rope_base)))
    angles = positions.astype(F32)[:, None] * frequency[None, :]
    cosine, sine = jnp.cos(angles), jnp.sin(angles)
    return (
        jnp.concatenate([cosine, cosine], axis=1),
        jnp.concatenate([-sine, sine], axis=1),
    )


def index_of(at):
    x_lo, y, z, core, x_hi = at["x"] % 2, at["y"], at["z"], at["core"], at["x"] // 2
    return (((x_lo * 4 + y) * 4 + z) * 2 + core) * 2 + x_hi


def ring_step(block, dims, step):
    pairs = []
    for n in range(128):
        at = {"x": n % 2 * 2 + n // 64, "core": n // 2 % 2, "z": n // 4 % 4, "y": n // 16 % 4}
        to = dict(at)
        dim = dims[at["core"]]
        to[dim] = (at[dim] + step) % 4
        pairs.append((index_of(at), index_of(to)))
    return lax.ppermute(block, AXES, pairs)


def ring(block, dims):
    middle = block.shape[0] // 2
    left, right = ring_step(block, dims, 1), ring_step(block, dims, -1)
    opposite = [ring_step(left[:middle], dims, 1), ring_step(right[middle:], dims, -1)]
    return jnp.concatenate([block, right, *opposite, left], axis=0)


def ringed_units(rows, x, y, z, core):
    count = rows.shape[0]
    stack = jnp.zeros((4 * count, rows.shape[1]), rows.dtype)
    for step in range(4):
        piece = rows if step == 0 else ring_step(rows, ("z", "z"), -step)
        at = lax.rem(z + step, 4) * count
        stack = lax.dynamic_update_slice(stack, piece, (at, jnp.int32(0)))
    units = ring(ring(stack, ("y", "x")), ("x", "y"))
    n = jnp.arange(16, dtype=jnp.int32)
    off_x, off_y = (n // 4 - x) % 4, (n % 4 - y) % 4
    slots = jnp.where(core == 0, off_x * 4 + off_y, off_y * 4 + off_x)
    return units.reshape(16, 4 * count, -1), slots


def quarter_rows(pieces):
    rows = pieces[0].shape[0]
    sides = [
        jnp.concatenate([p[:, s * p.shape[1] // 2 : (s + 1) * p.shape[1] // 2] for p in pieces], 1)
        for s in range(2)
    ]
    swapped = lax.all_to_all(jnp.stack(sides), "core", 0, 0, tiled=True)
    return swapped.reshape(2 * rows, -1)


def on_device(
    tokens,
    norm_gain,
    query_weight,
    key_matrix,
    value_matrix,
    out_weight,
    query_gain,
    key_gain,
    post_gain,
):
    core = lax.axis_index("core")
    side = lax.axis_index("x_hi")
    chip = lax.axis_index(CHIPS)
    full = lax.all_gather(
        quarter_rows([query_weight, out_weight]), GATHER, axis=0, tiled=True
    )
    place = [lax.axis_index(name) for name in ("x_hi", "x_lo", "y", "z")]
    units, slots = ringed_units(
        quarter_rows([key_matrix, value_matrix]),
        place[0] * 2 + place[1], place[2], place[3], core,
    )

    plain = tokens.astype(F32)
    mean_square = jnp.mean(plain * plain, axis=-1, keepdims=True)
    normed = (plain * lax.rsqrt(mean_square + epsilon) * norm_gain).astype(BF)
    other = lax.ppermute(normed, "core", [(0, 1), (1, 0)])
    x = jnp.concatenate(
        [jnp.where(core == 0, normed, other), jnp.where(core == 0, other, normed)], axis=0
    )
    row = jnp.arange(2 * BLOCK, dtype=jnp.int32)
    positions = (4 * chip + side) * BLOCK + row + (row // BLOCK) * BLOCK
    cosine, sine = rotations(positions)

    own = key_values(slots, x, units, key_gain.reshape(1, HEAD), cosine, sine)
    first, second = own[:BLOCK], own[BLOCK:]
    mine = jnp.where(side == 0, first, second)
    swap = jnp.where(side == 0, second, first)
    line = CHIPS + ("x_hi",)
    chips = 32
    prior = lax.ppermute(mine, line, [(i, i + 1) for i in range(2 * chips - 1)])
    gap = lax.ppermute(
        swap, line,
        [(2 * i + 1, 2 * i + 2) for i in range(chips - 1)]
        + [(2 * i, 2 * i + 3) for i in range(chips - 1)],
    )
    link = lax.ppermute(swap, "x_hi", [(0, 1), (1, 0)])
    behind = lax.ppermute(own, CHIPS, [(i, i + 1) for i in range(chips - 1)])
    full, prior, gap, link, behind = lax.optimization_barrier((full, prior, gap, link, behind))
    queries = projection(
        query_kernel, x, full, query_gain.reshape(1, HEAD), cosine, sine,
        lambda t: (t // 2, lax.rem(t, 2)),
    )
    later = (chip > 0).astype(jnp.int32)
    flags = jnp.stack([later, jnp.maximum(later, side), core]).astype(jnp.int32)
    attended = attention(flags, queries, own, behind, prior, gap, link)
    own0, send0 = out_projection(attended, full, 0)
    got0 = lax.ppermute(send0, "core", [(0, 1), (1, 0)])
    own1, send1 = out_projection(attended, full, 1)
    got1 = lax.ppermute(send1, "core", [(0, 1), (1, 0)])
    return ending(tokens, own0, own1, got0, got1, post_gain.reshape(1, WIDTH))


def solution(mesh):
    spread = Mesh(mesh.devices.reshape(2, 4, 4, 2, 2), AXES)
    whole = P(AXES, None)
    rows = P(AXES[:4], "x_hi")
    return jax.shard_map(
        on_device,
        mesh=spread,
        in_specs=(whole, P(), rows, rows, rows, rows, P(), P(), P()),
        out_specs=whole,
        check_vma=False,
    )
```

```python
import math

import jax
import jax.numpy as jnp
from jax import lax
from jax.experimental import pallas as pl
from jax.experimental.pallas import tpu as pltpu
from jax.sharding import Mesh, PartitionSpec as P

HEAD = 128
HALF = HEAD // 2
BLOCK = 256
WIDTH = 5376
AXES = ("x_lo", "y", "z", "core", "x_hi")
CHIPS = ("x_lo", "y", "z")
GATHER = ("x_hi", "x_lo", "y", "z")
epsilon = 1e-06
query_scale = 168.0 ** (-0.5) * math.log2(math.e)
rope_base = 10000.0
BF = jnp.bfloat16
F32 = jnp.float32
MIB = 1 << 20
SCALARS = pl.BlockSpec(memory_space=pltpu.SMEM)


def cost(flops, size, exps=0):
    return pl.CostEstimate(flops=int(flops), bytes_accessed=int(size), transcendentals=int(exps))


def params(mib):
    return pltpu.CompilerParams(vmem_limit_bytes=mib * MIB)


def turned(raw, gain, cosine, sine, scale):
    mean_square = jnp.mean(raw * raw, axis=-1, keepdims=True)
    unit = raw * (lax.rsqrt(mean_square + epsilon) * scale) * gain
    return unit * cosine + pltpu.roll(unit, HALF, axis=1) * sine


def key_value_kernel(x_ref, w_ref, gain_ref, cos_ref, sin_ref, out_ref):
    raw = jnp.dot(x_ref[...], w_ref[...], preferred_element_type=F32)

    @pl.when(pl.program_id(0) < 2)
    def _():
        for h in range(2):
            at = slice(h * HEAD, (h + 1) * HEAD)
            key = turned(raw[:, at], gain_ref[...], cos_ref[...], sin_ref[...], 1.0)
            out_ref[:, at] = key.astype(BF)

    @pl.when(pl.program_id(0) >= 2)
    def _():
        out_ref[...] = raw.astype(BF)


def query_kernel(x_ref, w_ref, gain_ref, cos_ref, sin_ref, out_ref):
    raw = jnp.dot(x_ref[...], w_ref[...], preferred_element_type=F32)
    for h in range(2):
        at = slice(h * HEAD, (h + 1) * HEAD)
        query = turned(raw[:, at], gain_ref[...], cos_ref[...], sin_ref[...], query_scale)
        out_ref[:, at] = query.astype(BF)


def chip_rows_kernel(core_ref, mine_ref, other_ref, out_ref):
    core = core_ref[0]
    for ref, which in ((mine_ref, core), (other_ref, 1 - core)):
        out_ref[pl.ds(pl.multiple_of(which * BLOCK, BLOCK), BLOCK), :] = ref[...]


def chip_rows(core, mine, other):
    whole = pl.BlockSpec(memory_space=pltpu.VMEM)
    return pl.pallas_call(
        chip_rows_kernel,
        out_shape=pltpu.VMEM((2 * BLOCK, WIDTH), BF),
        in_specs=[SCALARS, whole, whole],
        out_specs=whole,
        compiler_params=params(16),
        cost_estimate=cost(0, 12 * MIB),
    )(core.astype(jnp.int32).reshape(1), mine, other)


def projection(kernel, x, weights, gain, cosine, sine, where):
    rows = x.shape[0]
    whole = pl.BlockSpec(memory_space=pltpu.VMEM)
    return pl.pallas_call(
        kernel,
        out_shape=jax.ShapeDtypeStruct((rows, 1024), BF),
        grid=(4,),
        in_specs=[whole, pl.BlockSpec((WIDTH, 256), where), whole, whole, whole],
        out_specs=pl.BlockSpec((rows, 256), lambda t: (0, t)),
        compiler_params=params(20),
        cost_estimate=cost(2 * rows * WIDTH * 1024, 2 * WIDTH * 1536),
    )(x, weights, gain, cosine, sine)


def attend(query, keys, total):
    row = lax.rem(lax.broadcasted_iota(jnp.int32, (2 * BLOCK, BLOCK), 0), BLOCK)
    col = lax.broadcasted_iota(jnp.int32, (2 * BLOCK, BLOCK), 1)
    for key, value, count, edge in keys:
        score = lax.dot_general(query, key, (((1,), (1,)), ((), ())), preferred_element_type=F32)
        raised = jnp.exp2(score)
        if edge == "oldest":
            raised = jnp.where(col > row, raised, 0.0)
        if edge == "own":
            raised = jnp.where(col <= row, raised, 0.0)
        counted = jnp.concatenate([value, count], axis=1)
        total += jnp.dot(raised.astype(BF), counted, preferred_element_type=F32)
    return total


def counts(flag):
    lane = lax.broadcasted_iota(jnp.int32, (BLOCK, HEAD), 1)
    return jnp.where(lane == 0, flag.astype(F32), 0.0).astype(BF)


def both_heads(q_ref, part):
    at = slice(part * BLOCK, (part + 1) * BLOCK)
    return jnp.concatenate([q_ref[at, :HEAD], q_ref[at, HEAD:]], axis=0)


def near_kernel(flag_ref, q_ref, ok, ov, zk, zv, sum_ref):
    early, always = counts(flag_ref[0]), counts(jnp.int32(1))
    first, second = slice(0, BLOCK), slice(BLOCK, 2 * BLOCK)
    keys = (
        (
            (zk[first], zv[first], early, "oldest"),
            (zk[second], zv[second], early, ""),
            (ok[first], ov[first], always, "own"),
        ),
        (
            (zk[second], zv[second], early, "oldest"),
            (ok[first], ov[first], always, ""),
            (ok[second], ov[second], always, "own"),
        ),
    )
    for part in range(2):
        start = jnp.zeros((2 * BLOCK, 2 * HEAD), F32)
        sum_ref[0, part] = attend(both_heads(q_ref, part), keys[part], start)


def far_kernel(flag_ref, q_ref, sum_ref, pk, pv, gk, gv, lk, lv, out_ref):
    core = flag_ref[2]
    early, late, always = counts(flag_ref[0]), counts(flag_ref[1]), counts(jnp.int32(1))
    gap = (gk[...], gv[...], early, "")
    prior = (pk[...], pv[...], late, "")
    link = (lk[...], lv[...], always, "")
    for part, keys in enumerate(((gap, prior), (prior, link))):
        total = attend(both_heads(q_ref, part), keys, sum_ref[0, part])
        mixed = (total[:, :HEAD] / total[:, HEAD : HEAD + 1]).astype(BF)
        to = pl.multiple_of(lax.rem(part + core, 2) * BLOCK, BLOCK)
        out_ref[pl.ds(to, BLOCK), :HEAD] = mixed[:BLOCK]
        out_ref[pl.ds(to, BLOCK), HEAD:] = mixed[BLOCK:]


def head_pair(rows):
    return [
        pl.BlockSpec((rows, HEAD), lambda j: (0, j)),
        pl.BlockSpec((rows, HEAD), lambda j: (0, j + 4)),
    ]


QUERY_PAIR = pl.BlockSpec((2 * BLOCK, 2 * HEAD), lambda j: (0, j))
SUMS = pl.BlockSpec((1, 2, 2 * BLOCK, 2 * HEAD), lambda j: (j, 0, 0, 0))


def near_attention(flags, queries, own, behind):
    return pl.pallas_call(
        near_kernel,
        out_shape=jax.ShapeDtypeStruct((4, 2, 2 * BLOCK, 2 * HEAD), F32),
        grid=(4,),
        in_specs=[SCALARS, QUERY_PAIR] + head_pair(512) + head_pair(512),
        out_specs=SUMS,
        compiler_params=params(16),
        cost_estimate=cost(8 * 512 * 768 * 512, 6 * MIB, 8 * 512 * 768),
    )(flags, queries, own, own, behind, behind)


def far_attention(flags, queries, sums, prior, gap, link):
    return pl.pallas_call(
        far_kernel,
        out_shape=jax.ShapeDtypeStruct((2 * BLOCK, 1024), BF),
        grid=(4,),
        in_specs=[SCALARS, QUERY_PAIR, SUMS] + head_pair(256) * 3,
        out_specs=QUERY_PAIR,
        compiler_params=params(16),
        cost_estimate=cost(8 * 512 * 512 * 512, 6 * MIB, 8 * 512 * 512),
    )(flags, queries, sums, prior, prior, gap, gap, link, link)


def out_kernel(att_ref, low_ref, high_ref, own_ref, other_ref):
    dims = (((1,), (1,)), ((), ()))
    got = lax.dot_general(att_ref[:, :512], low_ref[...], dims, preferred_element_type=F32)
    got += lax.dot_general(att_ref[:, 512:], high_ref[...], dims, preferred_element_type=F32)
    own_ref[...] = got[:BLOCK]
    other_ref[...] = got[BLOCK:].astype(BF)


def out_projection(attended, weights, half):
    tile, steps = 896, 3
    first = half * steps
    return pl.pallas_call(
        out_kernel,
        out_shape=(
            jax.ShapeDtypeStruct((BLOCK, WIDTH // 2), F32),
            jax.ShapeDtypeStruct((BLOCK, WIDTH // 2), BF),
        ),
        grid=(steps,),
        in_specs=[
            pl.BlockSpec(memory_space=pltpu.VMEM),
            pl.BlockSpec((tile, 512), lambda i: (first + i, 0)),
            pl.BlockSpec((tile, 512), lambda i: (first + i + 2 * steps, 0)),
        ],
        out_specs=(
            pl.BlockSpec((BLOCK, tile), lambda i: (0, i)),
            pl.BlockSpec((BLOCK, tile), lambda i: (0, i)),
        ),
        compiler_params=params(16),
        cost_estimate=cost(2 * 512 * 1024 * WIDTH // 2, 10 * MIB),
    )(attended, weights, weights)


def end_kernel(tok_ref, own0, own1, got0, got1, gain_ref, out_ref):
    middle = WIDTH // 2
    left = own0[...] + got0[...].astype(F32)
    right = own1[...] + got1[...].astype(F32)
    square = jnp.sum(left * left, axis=-1, keepdims=True)
    square += jnp.sum(right * right, axis=-1, keepdims=True)
    factor = lax.rsqrt(square * (1.0 / WIDTH) + epsilon)
    for n, part in enumerate((left, right)):
        at = slice(n * middle, (n + 1) * middle)
        scaled = part * factor * gain_ref[:, at]
        out_ref[:, at] = (tok_ref[:, at].astype(F32) + scaled).astype(BF)


def ending(tokens, own0, own1, got0, got1, gain):
    rows = 64
    half = pl.BlockSpec((rows, WIDTH // 2), lambda i: (i, 0))
    wide = pl.BlockSpec((rows, WIDTH), lambda i: (i, 0))
    return pl.pallas_call(
        end_kernel,
        out_shape=jax.ShapeDtypeStruct((BLOCK, WIDTH), BF),
        grid=(BLOCK // rows,),
        in_specs=[wide, half, half, half, half, pl.BlockSpec((1, WIDTH), lambda i: (0, 0))],
        out_specs=wide,
        compiler_params=params(16),
        cost_estimate=cost(10 * BLOCK * WIDTH, 14 * MIB),
    )(tokens, own0, own1, got0, got1, gain)


def rotations(positions):
    exponents = jnp.arange(HALF, dtype=F32) * (2.0 / HEAD)
    frequency = jnp.exp(-exponents * jnp.log(jnp.float32(rope_base)))
    angles = positions.astype(F32)[:, None] * frequency[None, :]
    cosine, sine = jnp.cos(angles), jnp.sin(angles)
    return (
        jnp.concatenate([cosine, cosine], axis=1),
        jnp.concatenate([-sine, sine], axis=1),
    )


def quarter_rows(pieces):
    rows = pieces[0].shape[0]
    sides = [
        jnp.concatenate([p[:, s * p.shape[1] // 2 : (s + 1) * p.shape[1] // 2] for p in pieces], 1)
        for s in range(2)
    ]
    swapped = lax.all_to_all(jnp.stack(sides), "core", 0, 0, tiled=True)
    return swapped.reshape(2 * rows, -1)


def on_device(
    tokens,
    norm_gain,
    query_weight,
    key_matrix,
    value_matrix,
    out_weight,
    query_gain,
    key_gain,
    post_gain,
):
    core = lax.axis_index("core")
    side = lax.axis_index("x_hi")
    chip = lax.axis_index(CHIPS)
    full = lax.all_gather(
        quarter_rows([query_weight, key_matrix, value_matrix, out_weight]),
        GATHER,
        axis=0,
        tiled=True,
    )

    plain = tokens.astype(F32)
    mean_square = jnp.mean(plain * plain, axis=-1, keepdims=True)
    normed = (plain * lax.rsqrt(mean_square + epsilon) * norm_gain).astype(BF)
    other = lax.ppermute(normed, "core", [(0, 1), (1, 0)])
    x = chip_rows(core, normed, other)
    row = jnp.arange(2 * BLOCK, dtype=jnp.int32)
    positions = (4 * chip + side) * BLOCK + row + (row // BLOCK) * BLOCK
    cosine, sine = rotations(positions)


    own = projection(
        key_value_kernel, x, full, key_gain.reshape(1, HEAD), cosine, sine,
        lambda t: (lax.rem(t, 2), 2 + t // 2),
    )
    first, second = own[:BLOCK], own[BLOCK:]
    line = CHIPS + ("x_hi",)
    chips = 32
    swap = [(0, 1), (1, 0)]
    behind = lax.ppermute(own, CHIPS, [(i, i + 1) for i in range(chips - 1)])
    link = lax.ppermute(jnp.where(side == 0, second, first), "x_hi", swap)
    prior = lax.ppermute(
        jnp.where(side == 0, first, second), line, [(i, i + 1) for i in range(2 * chips - 1)]
    )
    queries = projection(
        query_kernel, x, full, query_gain.reshape(1, HEAD), cosine, sine,
        lambda t: (t // 2, lax.rem(t, 2)),
    )
    queries, behind = lax.optimization_barrier((queries, behind))
    gap = lax.ppermute(jnp.where(side == 0, behind[BLOCK:], behind[:BLOCK]), "x_hi", swap)
    later = (chip > 0).astype(jnp.int32)
    flags = jnp.stack([later, jnp.maximum(later, side), core]).astype(jnp.int32)
    sums = near_attention(flags, queries, own, behind)
    out_rows, _ = lax.optimization_barrier((full, own))
    out_rows = out_rows[:, 1024:]
    attended = far_attention(flags, queries, sums, prior, gap, link)
    own0, send0 = out_projection(attended, out_rows, 0)
    got0 = lax.ppermute(send0, "core", [(0, 1), (1, 0)])
    own1, send1 = out_projection(attended, out_rows, 1)
    got1 = lax.ppermute(send1, "core", [(0, 1), (1, 0)])
    return ending(tokens, own0, own1, got0, got1, post_gain.reshape(1, WIDTH))


def solution(mesh):
    spread = Mesh(mesh.devices.reshape(2, 4, 4, 2, 2), AXES)
    whole = P(AXES, None)
    rows = P(AXES[:4], "x_hi")
    return jax.shard_map(
        on_device,
        mesh=spread,
        in_specs=(whole, P(), rows, rows, rows, rows, P(), P(), P()),
        out_specs=whole,
        check_vma=False,
    )
```

```python
import math

import jax
import jax.numpy as jnp
from jax import lax
from jax.experimental import pallas as pl
from jax.experimental.pallas import tpu as pltpu
from jax.sharding import Mesh, PartitionSpec as P

HEAD = 128
HALF = HEAD // 2
BLOCK = 256
WIDTH = 5376
AXES = ("x_lo", "y", "z", "core", "x_hi")
CHIPS = ("x_lo", "y", "z")
GATHER = ("x_hi", "x_lo", "y", "z")
epsilon = 1e-06
query_scale = 168.0 ** (-0.5) * math.log2(math.e)
rope_base = 10000.0
BF = jnp.bfloat16
F32 = jnp.float32
MIB = 1 << 20
SCALARS = pl.BlockSpec(memory_space=pltpu.SMEM)


def cost(flops, size, exps=0):
    return pl.CostEstimate(flops=int(flops), bytes_accessed=int(size), transcendentals=int(exps))


def params(mib):
    return pltpu.CompilerParams(vmem_limit_bytes=mib * MIB)


def turned(raw, gain, cosine, sine, scale):
    mean_square = jnp.mean(raw * raw, axis=-1, keepdims=True)
    unit = raw * (lax.rsqrt(mean_square + epsilon) * scale) * gain
    return unit * cosine + pltpu.roll(unit, HALF, axis=1) * sine


def key_value_kernel(x_ref, low_ref, high_ref, gain_ref, cos_ref, sin_ref, out_ref, sum_ref):
    step = pl.program_id(0)
    terms = [
        jnp.dot(x_ref[...], ref[...], preferred_element_type=F32) for ref in (low_ref, high_ref)
    ]

    @pl.when(step == 0)
    def _():
        for n in range(2):
            sum_ref[n] = terms[n]

    @pl.when(step > 0)
    def _():
        for n in range(2):
            sum_ref[n] += terms[n]

    @pl.when(step == pl.num_programs(0) - 1)
    def _():
        for n in range(2):
            for h in range(2):
                raw = sum_ref[n, :, h * HEAD : (h + 1) * HEAD]
                key = turned(raw, gain_ref[...], cos_ref[...], sin_ref[...], 1.0)
                out_ref[:, (2 * n + h) * HEAD : (2 * n + h + 1) * HEAD] = key.astype(BF)
            out_ref[:, 512 + 256 * n : 768 + 256 * n] = sum_ref[n, :, 256:].astype(BF)


def key_values(x, weights, gain, cosine, sine):
    rows, steps = x.shape[0], 3
    depth = WIDTH // steps

    def whole(shape):
        return pl.BlockSpec(shape, lambda t: (0, 0))

    return pl.pallas_call(
        key_value_kernel,
        out_shape=jax.ShapeDtypeStruct((rows, 1024), BF),
        grid=(steps,),
        in_specs=[
            pl.BlockSpec((rows, depth), lambda t: (0, t)),
            pl.BlockSpec((depth, 512), lambda t: (t, 1)),
            pl.BlockSpec((depth, 512), lambda t: (t + steps, 1)),
            whole((1, HEAD)),
            whole((rows, HEAD)),
            whole((rows, HEAD)),
        ],
        out_specs=whole((rows, 1024)),
        scratch_shapes=[pltpu.VMEM((2, rows, 512), F32)],
        compiler_params=params(60),
        cost_estimate=cost(2 * rows * WIDTH * 1024, 2 * WIDTH * 1536),
    )(x, weights, weights, gain, cosine, sine)


def query_kernel(x_ref, w_ref, gain_ref, cos_ref, sin_ref, out_ref):
    raw = jnp.dot(x_ref[...], w_ref[...], preferred_element_type=F32)
    for h in range(2):
        at = slice(h * HEAD, (h + 1) * HEAD)
        query = turned(raw[:, at], gain_ref[...], cos_ref[...], sin_ref[...], query_scale)
        out_ref[:, at] = query.astype(BF)


def chip_rows_kernel(core_ref, mine_ref, other_ref, out_ref):
    core = core_ref[0]
    for ref, which in ((mine_ref, core), (other_ref, 1 - core)):
        out_ref[pl.ds(pl.multiple_of(which * BLOCK, BLOCK), BLOCK), :] = ref[...]


def chip_rows(core, mine, other):
    whole = pl.BlockSpec(memory_space=pltpu.VMEM)
    return pl.pallas_call(
        chip_rows_kernel,
        out_shape=jax.ShapeDtypeStruct((2 * BLOCK, WIDTH), BF),
        in_specs=[SCALARS, whole, whole],
        out_specs=whole,
        compiler_params=params(16),
        cost_estimate=cost(0, 12 * MIB),
    )(core.astype(jnp.int32).reshape(1), mine, other)


def projection(kernel, x, weights, gain, cosine, sine, where):
    rows = x.shape[0]
    whole = pl.BlockSpec(memory_space=pltpu.VMEM)
    return pl.pallas_call(
        kernel,
        out_shape=jax.ShapeDtypeStruct((rows, 1024), BF),
        grid=(4,),
        in_specs=[whole, pl.BlockSpec((WIDTH, 256), where), whole, whole, whole],
        out_specs=pl.BlockSpec((rows, 256), lambda t: (0, t)),
        compiler_params=params(20),
        cost_estimate=cost(2 * rows * WIDTH * 1024, 2 * WIDTH * 1536),
    )(x, weights, gain, cosine, sine)


def attend(query, keys, total):
    row = lax.rem(lax.broadcasted_iota(jnp.int32, (2 * BLOCK, BLOCK), 0), BLOCK)
    col = lax.broadcasted_iota(jnp.int32, (2 * BLOCK, BLOCK), 1)
    for key, value, count, edge in keys:
        score = lax.dot_general(query, key, (((1,), (1,)), ((), ())), preferred_element_type=F32)
        raised = jnp.exp2(score)
        if edge == "oldest":
            raised = jnp.where(col > row, raised, 0.0)
        if edge == "own":
            raised = jnp.where(col <= row, raised, 0.0)
        counted = jnp.concatenate([value, count], axis=1)
        total += jnp.dot(raised.astype(BF), counted, preferred_element_type=F32)
    return total


def counts(flag):
    lane = lax.broadcasted_iota(jnp.int32, (BLOCK, HEAD), 1)
    return jnp.where(lane == 0, flag.astype(F32), 0.0).astype(BF)


def both_heads(q_ref, part):
    at = slice(part * BLOCK, (part + 1) * BLOCK)
    return jnp.concatenate([q_ref[at, :HEAD], q_ref[at, HEAD:]], axis=0)


def near_kernel(flag_ref, q_ref, ok, ov, zk, zv, sum_ref):
    early, always = counts(flag_ref[0]), counts(jnp.int32(1))
    first, second = slice(0, BLOCK), slice(BLOCK, 2 * BLOCK)
    keys = (
        (
            (zk[first], zv[first], early, "oldest"),
            (zk[second], zv[second], early, ""),
            (ok[first], ov[first], always, "own"),
        ),
        (
            (zk[second], zv[second], early, "oldest"),
            (ok[first], ov[first], always, ""),
            (ok[second], ov[second], always, "own"),
        ),
    )
    for part in range(2):
        start = jnp.zeros((2 * BLOCK, 2 * HEAD), F32)
        sum_ref[0, part] = attend(both_heads(q_ref, part), keys[part], start)


def far_kernel(flag_ref, q_ref, sum_ref, nk, nv, ck, cv, out_ref):
    core, side = flag_ref[2], flag_ref[3]
    early, late, always = counts(flag_ref[0]), counts(flag_ref[1]), counts(jnp.int32(1))
    before = pl.ds(pl.multiple_of((1 - side) * BLOCK, BLOCK), BLOCK)
    beside = pl.ds(pl.multiple_of(side * BLOCK, BLOCK), BLOCK)
    gap = tuple(jnp.where(side == 0, n[beside], c[...]) for n, c in ((nk, ck), (nv, cv)))
    link = tuple(jnp.where(side == 0, c[...], n[beside]) for n, c in ((nk, ck), (nv, cv)))
    gap, link = gap + (early, ""), link + (always, "")
    prior = (nk[before], nv[before], late, "")
    for part, keys in enumerate(((gap, prior), (prior, link))):
        total = attend(both_heads(q_ref, part), keys, sum_ref[0, part])
        mixed = (total[:, :HEAD] / total[:, HEAD : HEAD + 1]).astype(BF)
        to = pl.multiple_of(lax.rem(part + core, 2) * BLOCK, BLOCK)
        out_ref[pl.ds(to, BLOCK), :HEAD] = mixed[:BLOCK]
        out_ref[pl.ds(to, BLOCK), HEAD:] = mixed[BLOCK:]


def head_pair(rows):
    return [
        pl.BlockSpec((rows, HEAD), lambda j: (0, j)),
        pl.BlockSpec((rows, HEAD), lambda j: (0, j + 4)),
    ]


QUERY_PAIR = pl.BlockSpec((2 * BLOCK, 2 * HEAD), lambda j: (0, j))
SUMS = pl.BlockSpec((1, 2, 2 * BLOCK, 2 * HEAD), lambda j: (j, 0, 0, 0))


def near_attention(flags, queries, own, behind):
    return pl.pallas_call(
        near_kernel,
        out_shape=jax.ShapeDtypeStruct((4, 2, 2 * BLOCK, 2 * HEAD), F32),
        grid=(4,),
        in_specs=[SCALARS, QUERY_PAIR] + head_pair(512) + head_pair(512),
        out_specs=SUMS,
        compiler_params=params(16),
        cost_estimate=cost(8 * 512 * 768 * 512, 6 * MIB, 8 * 512 * 768),
    )(flags, queries, own, own, behind, behind)


def far_attention(flags, queries, sums, near, cross):
    return pl.pallas_call(
        far_kernel,
        out_shape=jax.ShapeDtypeStruct((2 * BLOCK, 1024), BF),
        grid=(4,),
        in_specs=[SCALARS, QUERY_PAIR, SUMS] + head_pair(512) + head_pair(256),
        out_specs=QUERY_PAIR,
        compiler_params=params(16),
        cost_estimate=cost(8 * 512 * 512 * 512, 6 * MIB, 8 * 512 * 512),
    )(flags, queries, sums, near, near, cross, cross)


def out_kernel(att_ref, low_ref, high_ref, out_ref):
    dims = (((1,), (1,)), ((), ()))
    got = lax.dot_general(att_ref[:, :512], low_ref[...], dims, preferred_element_type=F32)
    got += lax.dot_general(att_ref[:, 512:], high_ref[...], dims, preferred_element_type=F32)
    out_ref[...] = got.astype(out_ref.dtype)


def out_projection(attended, weights, which, kind):
    tile, steps = 896, 6
    return pl.pallas_call(
        out_kernel,
        out_shape=jax.ShapeDtypeStruct((BLOCK, WIDTH), kind),
        grid=(steps,),
        in_specs=[
            pl.BlockSpec((BLOCK, 1024), lambda i: (which, 0)),
            pl.BlockSpec((tile, 512), lambda i: (i, 0)),
            pl.BlockSpec((tile, 512), lambda i: (i + steps, 0)),
        ],
        out_specs=pl.BlockSpec((BLOCK, tile), lambda i: (0, i)),
        compiler_params=params(16),
        cost_estimate=cost(2 * BLOCK * 1024 * WIDTH, 15 * MIB),
    )(attended, weights, weights)


def end_kernel(tok_ref, own_ref, got_ref, gain_ref, out_ref):
    whole = own_ref[...] + got_ref[...].astype(F32)
    mean_square = jnp.mean(whole * whole, axis=-1, keepdims=True)
    scaled = whole * lax.rsqrt(mean_square + epsilon) * gain_ref[...]
    out_ref[...] = (tok_ref[...].astype(F32) + scaled).astype(BF)


def ending(tokens, own, got, gain):
    rows = 64
    wide = pl.BlockSpec((rows, WIDTH), lambda i: (i, 0))
    return pl.pallas_call(
        end_kernel,
        out_shape=jax.ShapeDtypeStruct((BLOCK, WIDTH), BF),
        grid=(BLOCK // rows,),
        in_specs=[wide, wide, wide, pl.BlockSpec((1, WIDTH), lambda i: (0, 0))],
        out_specs=wide,
        compiler_params=params(24),
        cost_estimate=cost(10 * BLOCK * WIDTH, 14 * MIB),
    )(tokens, own, got, gain)


def rotations(positions):
    exponents = jnp.arange(HALF, dtype=F32) * (2.0 / HEAD)
    frequency = jnp.exp(-exponents * jnp.log(jnp.float32(rope_base)))
    angles = positions.astype(F32)[:, None] * frequency[None, :]
    cosine, sine = jnp.cos(angles), jnp.sin(angles)
    return (
        jnp.concatenate([cosine, cosine], axis=1),
        jnp.concatenate([-sine, sine], axis=1),
    )


def pack_kernel(core_ref, q_ref, k_ref, v_ref, o_ref, keep_ref, send_ref):
    def pack(to_ref, side):
        at = 0
        for ref in (q_ref, k_ref, v_ref, o_ref):
            width = ref.shape[1] // 2
            to_ref[:, at : at + width] = ref[:, side * width : (side + 1) * width]
            at += width

    for core in range(2):

        @pl.when(core_ref[0] == core)
        def _():
            pack(keep_ref, core)
            pack(send_ref, 1 - core)


def chip_weights(core, q, k, v, o):
    rows = q.shape[0]
    whole = pl.BlockSpec(memory_space=pltpu.VMEM)
    keep, send = pl.pallas_call(
        pack_kernel,
        out_shape=(jax.ShapeDtypeStruct((rows, 1536), BF),) * 2,
        in_specs=[SCALARS, whole, whole, whole, whole],
        out_specs=(whole, whole),
        compiler_params=params(60),
        cost_estimate=cost(0, 1 * MIB),
    )(core.astype(jnp.int32).reshape(1), q, k, v, o)
    got = lax.ppermute(send, "core", [(0, 1), (1, 0)])
    first, second = jnp.where(core == 0, keep, got), jnp.where(core == 0, got, keep)
    return jnp.concatenate([first, second], axis=0)


def on_device(
    tokens,
    norm_gain,
    query_weight,
    key_matrix,
    value_matrix,
    out_weight,
    query_gain,
    key_gain,
    post_gain,
):
    core = lax.axis_index("core")
    side = lax.axis_index("x_hi")
    chip = lax.axis_index(CHIPS)
    full = lax.all_gather(
        chip_weights(core, query_weight, key_matrix, value_matrix, out_weight),
        GATHER,
        axis=0,
        tiled=True,
    )

    plain = tokens.astype(F32)
    mean_square = jnp.mean(plain * plain, axis=-1, keepdims=True)
    normed = (plain * lax.rsqrt(mean_square + epsilon) * norm_gain).astype(BF)
    other = lax.ppermute(normed, "core", [(0, 1), (1, 0)])
    x = chip_rows(core, normed, other)
    row = jnp.arange(2 * BLOCK, dtype=jnp.int32)
    positions = (4 * chip + side) * BLOCK + row + (row // BLOCK) * BLOCK
    cosine, sine = rotations(positions)


    own = key_values(x, full, key_gain.reshape(1, HEAD), cosine, sine)
    line = CHIPS + ("x_hi",)
    chips = 32
    single = jnp.where(side == 0, own[BLOCK:], own[:BLOCK])
    near = lax.ppermute(own, line, [(i, i + 1) for i in range(2 * chips - 1)])
    behind = lax.ppermute(own, CHIPS, [(i, i + 1) for i in range(chips - 1)])
    cross = lax.ppermute(
        single, line,
        [(2 * i + 1, 2 * i) for i in range(chips)]
        + [(2 * i, 2 * i + 3) for i in range(chips - 1)],
    )
    queries = projection(
        query_kernel, x, full, query_gain.reshape(1, HEAD), cosine, sine,
        lambda t: (t // 2, lax.rem(t, 2)),
    )
    later = (chip > 0).astype(jnp.int32)
    flags = jnp.stack([later, jnp.maximum(later, side), core, side]).astype(jnp.int32)
    sums = near_attention(flags, queries, own, behind)
    out_rows, _ = lax.optimization_barrier((full, own))
    out_rows = out_rows[:, 1024:]
    attended = far_attention(flags, queries, sums, near, cross)
    theirs = out_projection(attended, out_rows, 1, BF)
    got = lax.ppermute(theirs, "core", [(0, 1), (1, 0)])
    ours = out_projection(attended, out_rows, 0, F32)
    return ending(tokens, ours, got, post_gain.reshape(1, WIDTH))


def solution(mesh):
    spread = Mesh(mesh.devices.reshape(2, 4, 4, 2, 2), AXES)
    whole = P(AXES, None)
    rows = P(AXES[:4], "x_hi")
    return jax.shard_map(
        on_device,
        mesh=spread,
        in_specs=(whole, P(), rows, rows, rows, rows, P(), P(), P()),
        out_specs=whole,
        check_vma=False,
    )
```

```python
import math

import jax
import jax.numpy as jnp
from jax import lax
from jax.experimental import pallas as pl
from jax.experimental.pallas import tpu as pltpu
from jax.sharding import Mesh, PartitionSpec as P

HEAD = 128
HALF = HEAD // 2
BLOCK = 256
WIDTH = 5376
AXES = ("x_lo", "y", "z", "core", "x_hi")
CHIPS = ("x_lo", "y", "z")
GATHER = ("x_hi", "x_lo", "y", "z")
epsilon = 1e-06
query_scale = 168.0 ** (-0.5) * math.log2(math.e)
rope_base = 10000.0
BF = jnp.bfloat16
F32 = jnp.float32
MIB = 1 << 20
SCALARS = pl.BlockSpec(memory_space=pltpu.SMEM)


def cost(flops, size, exps=0):
    return pl.CostEstimate(flops=int(flops), bytes_accessed=int(size), transcendentals=int(exps))


def params(mib):
    return pltpu.CompilerParams(vmem_limit_bytes=mib * MIB)


def turned(raw, gain, cosine, sine, scale):
    mean_square = jnp.mean(raw * raw, axis=-1, keepdims=True)
    unit = raw * (lax.rsqrt(mean_square + epsilon) * scale) * gain
    return unit * cosine + pltpu.roll(unit, HALF, axis=1) * sine


def key_value_kernel(x_ref, low_ref, high_ref, gain_ref, cos_ref, sin_ref, out_ref, sum_ref):
    step = pl.program_id(0)
    terms = [
        jnp.dot(x_ref[...], ref[...], preferred_element_type=F32) for ref in (low_ref, high_ref)
    ]

    @pl.when(step == 0)
    def _():
        for n in range(2):
            sum_ref[n] = terms[n]

    @pl.when(step > 0)
    def _():
        for n in range(2):
            sum_ref[n] += terms[n]

    @pl.when(step == pl.num_programs(0) - 1)
    def _():
        for n in range(2):
            for h in range(2):
                raw = sum_ref[n, :, h * HEAD : (h + 1) * HEAD]
                key = turned(raw, gain_ref[...], cos_ref[...], sin_ref[...], 1.0)
                out_ref[:, (2 * n + h) * HEAD : (2 * n + h + 1) * HEAD] = key.astype(BF)
            out_ref[:, 512 + 256 * n : 768 + 256 * n] = sum_ref[n, :, 256:].astype(BF)


def key_values(x, weights, gain, cosine, sine):
    rows, steps = x.shape[0], 3
    depth = WIDTH // steps

    def whole(shape):
        return pl.BlockSpec(shape, lambda t: (0, 0))

    return pl.pallas_call(
        key_value_kernel,
        out_shape=jax.ShapeDtypeStruct((rows, 1024), BF),
        grid=(steps,),
        in_specs=[
            pl.BlockSpec((rows, depth), lambda t: (0, t)),
            pl.BlockSpec((depth, 512), lambda t: (t, 1)),
            pl.BlockSpec((depth, 512), lambda t: (t + steps, 1)),
            whole((1, HEAD)),
            whole((rows, HEAD)),
            whole((rows, HEAD)),
        ],
        out_specs=whole((rows, 1024)),
        scratch_shapes=[pltpu.VMEM((2, rows, 512), F32)],
        compiler_params=params(60),
        cost_estimate=cost(2 * rows * WIDTH * 1024, 2 * WIDTH * 1536),
    )(x, weights, weights, gain, cosine, sine)


def query_kernel(x_ref, w_ref, gain_ref, cos_ref, sin_ref, out_ref):
    raw = jnp.dot(x_ref[...], w_ref[...], preferred_element_type=F32)
    for h in range(2):
        at = slice(h * HEAD, (h + 1) * HEAD)
        query = turned(raw[:, at], gain_ref[...], cos_ref[...], sin_ref[...], query_scale)
        out_ref[:, at] = query.astype(BF)


def chip_rows_kernel(core_ref, mine_ref, other_ref, out_ref):
    core = core_ref[0]
    for ref, which in ((mine_ref, core), (other_ref, 1 - core)):
        out_ref[pl.ds(pl.multiple_of(which * BLOCK, BLOCK), BLOCK), :] = ref[...]


def chip_rows(core, mine, other):
    whole = pl.BlockSpec(memory_space=pltpu.VMEM)
    return pl.pallas_call(
        chip_rows_kernel,
        out_shape=jax.ShapeDtypeStruct((2 * BLOCK, WIDTH), BF),
        in_specs=[SCALARS, whole, whole],
        out_specs=whole,
        compiler_params=params(16),
        cost_estimate=cost(0, 12 * MIB),
    )(core.astype(jnp.int32).reshape(1), mine, other)


def projection(kernel, x, weights, gain, cosine, sine, where):
    rows = x.shape[0]
    whole = pl.BlockSpec(memory_space=pltpu.VMEM)
    return pl.pallas_call(
        kernel,
        out_shape=jax.ShapeDtypeStruct((rows, 1024), BF),
        grid=(4,),
        in_specs=[whole, pl.BlockSpec((WIDTH, 256), where), whole, whole, whole],
        out_specs=pl.BlockSpec((rows, 256), lambda t: (0, t)),
        compiler_params=params(20),
        cost_estimate=cost(2 * rows * WIDTH * 1024, 2 * WIDTH * 1536),
    )(x, weights, gain, cosine, sine)


def attend(query, keys, total):
    row = lax.rem(lax.broadcasted_iota(jnp.int32, (2 * BLOCK, BLOCK), 0), BLOCK)
    col = lax.broadcasted_iota(jnp.int32, (2 * BLOCK, BLOCK), 1)
    for key, value, count, edge in keys:
        score = lax.dot_general(query, key, (((1,), (1,)), ((), ())), preferred_element_type=F32)
        raised = jnp.exp2(score)
        if edge == "oldest":
            raised = jnp.where(col > row, raised, 0.0)
        if edge == "own":
            raised = jnp.where(col <= row, raised, 0.0)
        counted = jnp.concatenate([value, count], axis=1)
        total += jnp.dot(raised.astype(BF), counted, preferred_element_type=F32)
    return total


def counts(flag):
    lane = lax.broadcasted_iota(jnp.int32, (BLOCK, HEAD), 1)
    return jnp.where(lane == 0, flag.astype(F32), 0.0).astype(BF)


def both_heads(q_ref, part):
    at = slice(part * BLOCK, (part + 1) * BLOCK)
    return jnp.concatenate([q_ref[at, :HEAD], q_ref[at, HEAD:]], axis=0)


def near_kernel(flag_ref, q_ref, ok, ov, zk, zv, sum_ref):
    early, always = counts(flag_ref[0]), counts(jnp.int32(1))
    first, second = slice(0, BLOCK), slice(BLOCK, 2 * BLOCK)
    keys = (
        (
            (zk[first], zv[first], early, "oldest"),
            (zk[second], zv[second], early, ""),
            (ok[first], ov[first], always, "own"),
        ),
        (
            (zk[second], zv[second], early, "oldest"),
            (ok[first], ov[first], always, ""),
            (ok[second], ov[second], always, "own"),
        ),
    )
    for part in range(2):
        start = jnp.zeros((2 * BLOCK, 2 * HEAD), F32)
        sum_ref[0, part] = attend(both_heads(q_ref, part), keys[part], start)


def far_kernel(flag_ref, q_ref, sum_ref, nk, nv, ck, cv, out_ref):
    core, side = flag_ref[2], flag_ref[3]
    early, late, always = counts(flag_ref[0]), counts(flag_ref[1]), counts(jnp.int32(1))
    before = pl.ds(pl.multiple_of((1 - side) * BLOCK, BLOCK), BLOCK)
    beside = pl.ds(pl.multiple_of(side * BLOCK, BLOCK), BLOCK)
    gap = tuple(jnp.where(side == 0, n[beside], c[...]) for n, c in ((nk, ck), (nv, cv)))
    link = tuple(jnp.where(side == 0, c[...], n[beside]) for n, c in ((nk, ck), (nv, cv)))
    gap, link = gap + (early, ""), link + (always, "")
    prior = (nk[before], nv[before], late, "")
    for part, keys in enumerate(((gap, prior), (prior, link))):
        total = attend(both_heads(q_ref, part), keys, sum_ref[0, part])
        mixed = (total[:, :HEAD] / total[:, HEAD : HEAD + 1]).astype(BF)
        to = pl.multiple_of(lax.rem(part + core, 2) * BLOCK, BLOCK)
        out_ref[pl.ds(to, BLOCK), :HEAD] = mixed[:BLOCK]
        out_ref[pl.ds(to, BLOCK), HEAD:] = mixed[BLOCK:]


def head_pair(rows):
    return [
        pl.BlockSpec((rows, HEAD), lambda j: (0, j)),
        pl.BlockSpec((rows, HEAD), lambda j: (0, j + 4)),
    ]


QUERY_PAIR = pl.BlockSpec((2 * BLOCK, 2 * HEAD), lambda j: (0, j))
SUMS = pl.BlockSpec((1, 2, 2 * BLOCK, 2 * HEAD), lambda j: (j, 0, 0, 0))


def near_attention(flags, queries, own, behind):
    return pl.pallas_call(
        near_kernel,
        out_shape=jax.ShapeDtypeStruct((4, 2, 2 * BLOCK, 2 * HEAD), F32),
        grid=(4,),
        in_specs=[SCALARS, QUERY_PAIR] + head_pair(512) + head_pair(512),
        out_specs=SUMS,
        compiler_params=params(16),
        cost_estimate=cost(8 * 512 * 768 * 512, 6 * MIB, 8 * 512 * 768),
    )(flags, queries, own, own, behind, behind)


def far_attention(flags, queries, sums, near, cross):
    return pl.pallas_call(
        far_kernel,
        out_shape=jax.ShapeDtypeStruct((2 * BLOCK, 1024), BF),
        grid=(4,),
        in_specs=[SCALARS, QUERY_PAIR, SUMS] + head_pair(512) + head_pair(256),
        out_specs=QUERY_PAIR,
        compiler_params=params(16),
        cost_estimate=cost(8 * 512 * 512 * 512, 6 * MIB, 8 * 512 * 512),
    )(flags, queries, sums, near, near, cross, cross)


OUT_TILE = 1792


def out_kernel(att_ref, weight_ref, out_ref):
    dims = (((1,), (1,)), ((), ()))
    at = pl.multiple_of(pl.program_id(0) * OUT_TILE, 128)
    got = lax.dot_general(
        att_ref[:, :512], weight_ref[pl.ds(at, OUT_TILE), :], dims, preferred_element_type=F32
    )
    got += lax.dot_general(
        att_ref[:, 512:], weight_ref[pl.ds(at + WIDTH, OUT_TILE), :], dims,
        preferred_element_type=F32,
    )
    out_ref[...] = got.astype(out_ref.dtype)


def out_projection(attended, weights, which, kind):
    return pl.pallas_call(
        out_kernel,
        out_shape=jax.ShapeDtypeStruct((BLOCK, WIDTH), kind),
        grid=(WIDTH // OUT_TILE,),
        in_specs=[
            pl.BlockSpec((BLOCK, 1024), lambda i: (which, 0)),
            pl.BlockSpec(memory_space=pltpu.VMEM),
        ],
        out_specs=pl.BlockSpec((BLOCK, OUT_TILE), lambda i: (0, i)),
        compiler_params=params(24),
        cost_estimate=cost(2 * BLOCK * 1024 * WIDTH, 15 * MIB),
    )(attended, weights)


def end_kernel(tok_ref, own_ref, got_ref, gain_ref, out_ref):
    whole = own_ref[...] + got_ref[...].astype(F32)
    mean_square = jnp.mean(whole * whole, axis=-1, keepdims=True)
    scaled = whole * lax.rsqrt(mean_square + epsilon) * gain_ref[...]
    out_ref[...] = (tok_ref[...].astype(F32) + scaled).astype(BF)


def ending(tokens, own, got, gain):
    rows = 128
    wide = pl.BlockSpec((rows, WIDTH), lambda i: (i, 0))
    return pl.pallas_call(
        end_kernel,
        out_shape=jax.ShapeDtypeStruct((BLOCK, WIDTH), BF),
        grid=(BLOCK // rows,),
        in_specs=[wide, wide, wide, pl.BlockSpec((1, WIDTH), lambda i: (0, 0))],
        out_specs=wide,
        compiler_params=params(24),
        cost_estimate=cost(10 * BLOCK * WIDTH, 14 * MIB),
    )(tokens, own, got, gain)


def rotations(positions):
    exponents = jnp.arange(HALF, dtype=F32) * (2.0 / HEAD)
    frequency = jnp.exp(-exponents * jnp.log(jnp.float32(rope_base)))
    angles = positions.astype(F32)[:, None] * frequency[None, :]
    cosine, sine = jnp.cos(angles), jnp.sin(angles)
    return (
        jnp.concatenate([cosine, cosine], axis=1),
        jnp.concatenate([-sine, sine], axis=1),
    )


def pack_kernel(core_ref, q_ref, k_ref, v_ref, o_ref, keep_ref, send_ref):
    def pack(to_ref, side):
        at = 0
        for ref in (q_ref, k_ref, v_ref, o_ref):
            width = ref.shape[1] // 2
            to_ref[:, at : at + width] = ref[:, side * width : (side + 1) * width]
            at += width

    for core in range(2):

        @pl.when(core_ref[0] == core)
        def _():
            pack(keep_ref, core)
            pack(send_ref, 1 - core)


def chip_weights(core, q, k, v, o):
    rows = q.shape[0]
    whole = pl.BlockSpec(memory_space=pltpu.VMEM)
    keep, send = pl.pallas_call(
        pack_kernel,
        out_shape=(jax.ShapeDtypeStruct((rows, 1536), BF),) * 2,
        in_specs=[SCALARS, whole, whole, whole, whole],
        out_specs=(whole, whole),
        compiler_params=params(60),
        cost_estimate=cost(0, 1 * MIB),
    )(core.astype(jnp.int32).reshape(1), q, k, v, o)
    got = lax.ppermute(send, "core", [(0, 1), (1, 0)])
    first, second = jnp.where(core == 0, keep, got), jnp.where(core == 0, got, keep)
    return jnp.concatenate([first, second], axis=0)


def on_device(
    tokens,
    norm_gain,
    query_weight,
    key_matrix,
    value_matrix,
    out_weight,
    query_gain,
    key_gain,
    post_gain,
):
    core = lax.axis_index("core")
    side = lax.axis_index("x_hi")
    chip = lax.axis_index(CHIPS)
    full = lax.all_gather(
        chip_weights(core, query_weight, key_matrix, value_matrix, out_weight),
        GATHER,
        axis=0,
        tiled=True,
    )

    plain = tokens.astype(F32)
    mean_square = jnp.mean(plain * plain, axis=-1, keepdims=True)
    normed = (plain * lax.rsqrt(mean_square + epsilon) * norm_gain).astype(BF)
    other = lax.ppermute(normed, "core", [(0, 1), (1, 0)])
    x = chip_rows(core, normed, other)
    row = jnp.arange(2 * BLOCK, dtype=jnp.int32)
    positions = (4 * chip + side) * BLOCK + row + (row // BLOCK) * BLOCK
    cosine, sine = rotations(positions)


    own = key_values(x, full, key_gain.reshape(1, HEAD), cosine, sine)
    line = CHIPS + ("x_hi",)
    chips = 32
    single = jnp.where(side == 0, own[BLOCK:], own[:BLOCK])
    near = lax.ppermute(own, line, [(i, i + 1) for i in range(2 * chips - 1)])
    behind = lax.ppermute(own, CHIPS, [(i, i + 1) for i in range(chips - 1)])
    cross = lax.ppermute(
        single, line,
        [(2 * i + 1, 2 * i) for i in range(chips)]
        + [(2 * i, 2 * i + 3) for i in range(chips - 1)],
    )
    queries = projection(
        query_kernel, x, full, query_gain.reshape(1, HEAD), cosine, sine,
        lambda t: (t // 2, lax.rem(t, 2)),
    )
    later = (chip > 0).astype(jnp.int32)
    flags = jnp.stack([later, jnp.maximum(later, side), core, side]).astype(jnp.int32)
    sums = near_attention(flags, queries, own, behind)
    out_rows, _ = lax.optimization_barrier((full, own))
    out_rows = out_rows[:, 1024:]
    attended = far_attention(flags, queries, sums, near, cross)
    theirs = out_projection(attended, out_rows, 1, BF)
    got = lax.ppermute(theirs, "core", [(0, 1), (1, 0)])
    ours = out_projection(attended, out_rows, 0, F32)
    return ending(tokens, ours, got, post_gain.reshape(1, WIDTH))


def solution(mesh):
    spread = Mesh(mesh.devices.reshape(2, 4, 4, 2, 2), AXES)
    whole = P(AXES, None)
    rows = P(AXES[:4], "x_hi")
    return jax.shard_map(
        on_device,
        mesh=spread,
        in_specs=(whole, P(), rows, rows, rows, rows, P(), P(), P()),
        out_specs=whole,
        check_vma=False,
    )
```

```python
import math

import jax
import jax.numpy as jnp
from jax import lax
from jax.experimental import pallas as pl
from jax.experimental.pallas import tpu as pltpu
from jax.sharding import Mesh, PartitionSpec as P

HEAD = 128
HALF = HEAD // 2
BLOCK = 256
WIDTH = 5376
AXES = ("x_lo", "y", "z", "core", "x_hi")
CHIPS = ("x_lo", "y", "z")
GATHER = ("x_hi", "x_lo", "y", "z")
epsilon = 1e-06
query_scale = 168.0 ** (-0.5) * math.log2(math.e)
rope_base = 10000.0
BF = jnp.bfloat16
F32 = jnp.float32
MIB = 1 << 20
SCALARS = pl.BlockSpec(memory_space=pltpu.SMEM)


def cost(flops, size, exps=0):
    return pl.CostEstimate(flops=int(flops), bytes_accessed=int(size), transcendentals=int(exps))


def params(mib):
    return pltpu.CompilerParams(vmem_limit_bytes=mib * MIB)


def turned(raw, gain, cosine, sine, scale):
    mean_square = jnp.mean(raw * raw, axis=-1, keepdims=True)
    unit = raw * (lax.rsqrt(mean_square + epsilon) * scale) * gain
    return unit * cosine + pltpu.roll(unit, HALF, axis=1) * sine


def key_value_kernel(x_ref, low_ref, high_ref, gain_ref, cos_ref, sin_ref, out_ref, sum_ref):
    step = pl.program_id(0)
    terms = [
        jnp.dot(x_ref[...], ref[...], preferred_element_type=F32) for ref in (low_ref, high_ref)
    ]

    @pl.when(step == 0)
    def _():
        for n in range(2):
            sum_ref[n] = terms[n]

    @pl.when(step > 0)
    def _():
        for n in range(2):
            sum_ref[n] += terms[n]

    @pl.when(step == pl.num_programs(0) - 1)
    def _():
        for n in range(2):
            for h in range(2):
                raw = sum_ref[n, :, h * HEAD : (h + 1) * HEAD]
                key = turned(raw, gain_ref[...], cos_ref[...], sin_ref[...], 1.0)
                out_ref[:, (2 * n + h) * HEAD : (2 * n + h + 1) * HEAD] = key.astype(BF)
            out_ref[:, 512 + 256 * n : 768 + 256 * n] = sum_ref[n, :, 256:].astype(BF)


def key_values(x, weights, gain, cosine, sine):
    rows, steps = x.shape[0], 3
    depth = WIDTH // steps

    def whole(shape):
        return pl.BlockSpec(shape, lambda t: (0, 0))

    return pl.pallas_call(
        key_value_kernel,
        out_shape=jax.ShapeDtypeStruct((rows, 1024), BF),
        grid=(steps,),
        in_specs=[
            pl.BlockSpec((rows, depth), lambda t: (0, t)),
            pl.BlockSpec((depth, 512), lambda t: (t, 1)),
            pl.BlockSpec((depth, 512), lambda t: (t + steps, 1)),
            whole((1, HEAD)),
            whole((rows, HEAD)),
            whole((rows, HEAD)),
        ],
        out_specs=whole((rows, 1024)),
        scratch_shapes=[pltpu.VMEM((2, rows, 512), F32)],
        compiler_params=params(60),
        cost_estimate=cost(2 * rows * WIDTH * 1024, 2 * WIDTH * 1536),
    )(x, weights, weights, gain, cosine, sine)


def query_kernel(x_ref, w_ref, gain_ref, cos_ref, sin_ref, out_ref):
    raw = jnp.dot(x_ref[...], w_ref[...], preferred_element_type=F32)
    for h in range(2):
        at = slice(h * HEAD, (h + 1) * HEAD)
        query = turned(raw[:, at], gain_ref[...], cos_ref[...], sin_ref[...], query_scale)
        out_ref[:, at] = query.astype(BF)


def chip_rows_kernel(core_ref, mine_ref, other_ref, out_ref):
    core = core_ref[0]
    for ref, which in ((mine_ref, core), (other_ref, 1 - core)):
        out_ref[pl.ds(pl.multiple_of(which * BLOCK, BLOCK), BLOCK), :] = ref[...]


def chip_rows(core, mine, other):
    whole = pl.BlockSpec(memory_space=pltpu.VMEM)
    return pl.pallas_call(
        chip_rows_kernel,
        out_shape=jax.ShapeDtypeStruct((2 * BLOCK, WIDTH), BF),
        in_specs=[SCALARS, whole, whole],
        out_specs=whole,
        compiler_params=params(16),
        cost_estimate=cost(0, 12 * MIB),
    )(core.astype(jnp.int32).reshape(1), mine, other)


def projection(kernel, x, weights, gain, cosine, sine, where):
    rows = x.shape[0]
    whole = pl.BlockSpec(memory_space=pltpu.VMEM)
    return pl.pallas_call(
        kernel,
        out_shape=jax.ShapeDtypeStruct((rows, 1024), BF),
        grid=(4,),
        in_specs=[whole, pl.BlockSpec((WIDTH, 256), where), whole, whole, whole],
        out_specs=pl.BlockSpec((rows, 256), lambda t: (0, t)),
        compiler_params=params(20),
        cost_estimate=cost(2 * rows * WIDTH * 1024, 2 * WIDTH * 1536),
    )(x, weights, gain, cosine, sine)


def attend(query, keys, total):
    row = lax.rem(lax.broadcasted_iota(jnp.int32, (2 * BLOCK, BLOCK), 0), BLOCK)
    col = lax.broadcasted_iota(jnp.int32, (2 * BLOCK, BLOCK), 1)
    for key, value, count, edge in keys:
        score = lax.dot_general(query, key, (((1,), (1,)), ((), ())), preferred_element_type=F32)
        raised = jnp.exp2(score)
        if edge == "oldest":
            raised = jnp.where(col > row, raised, 0.0)
        if edge == "own":
            raised = jnp.where(col <= row, raised, 0.0)
        counted = jnp.concatenate([value, count], axis=1)
        total += jnp.dot(raised.astype(BF), counted, preferred_element_type=F32)
    return total


def counts(flag):
    lane = lax.broadcasted_iota(jnp.int32, (BLOCK, HEAD), 1)
    return jnp.where(lane == 0, flag.astype(F32), 0.0).astype(BF)


def both_heads(q_ref, part):
    at = slice(part * BLOCK, (part + 1) * BLOCK)
    return jnp.concatenate([q_ref[at, :HEAD], q_ref[at, HEAD:]], axis=0)


def near_kernel(flag_ref, q_ref, ok, ov, zk, zv, sum_ref):
    early, always = counts(flag_ref[0]), counts(jnp.int32(1))
    first, second = slice(0, BLOCK), slice(BLOCK, 2 * BLOCK)
    keys = (
        (
            (zk[first], zv[first], early, "oldest"),
            (zk[second], zv[second], early, ""),
            (ok[first], ov[first], always, "own"),
        ),
        (
            (zk[second], zv[second], early, "oldest"),
            (ok[first], ov[first], always, ""),
            (ok[second], ov[second], always, "own"),
        ),
    )
    for part in range(2):
        start = jnp.zeros((2 * BLOCK, 2 * HEAD), F32)
        sum_ref[0, part] = attend(both_heads(q_ref, part), keys[part], start)


def far_kernel(flag_ref, q_ref, sum_ref, nk, nv, ck, cv, out_ref):
    core, side = flag_ref[2], flag_ref[3]
    early, late, always = counts(flag_ref[0]), counts(flag_ref[1]), counts(jnp.int32(1))
    before = pl.ds(pl.multiple_of((1 - side) * BLOCK, BLOCK), BLOCK)
    beside = pl.ds(pl.multiple_of(side * BLOCK, BLOCK), BLOCK)
    for head in range(2):
        lanes = slice(head * HEAD, (head + 1) * HEAD)
        wide = slice(head * 2 * HEAD, (head + 1) * 2 * HEAD)
        gap = tuple(
            jnp.where(side == 0, n[beside, lanes], c[:, lanes]) for n, c in ((nk, ck), (nv, cv))
        )
        link = tuple(
            jnp.where(side == 0, c[:, lanes], n[beside, lanes]) for n, c in ((nk, ck), (nv, cv))
        )
        gap, link = gap + (early, ""), link + (always, "")
        prior = (nk[before, lanes], nv[before, lanes], late, "")
        for part, keys in enumerate(((gap, prior), (prior, link))):
            query = both_heads(q_ref.at[:, wide], part)
            total = attend(query, keys, sum_ref[head, part])
            mixed = (total[:, :HEAD] / total[:, HEAD : HEAD + 1]).astype(BF)
            to = pl.ds(pl.multiple_of(lax.rem(part + core, 2) * BLOCK, BLOCK), BLOCK)
            out_ref[to, wide] = jnp.concatenate([mixed[:BLOCK], mixed[BLOCK:]], axis=1)


def head_pair(rows):
    return [
        pl.BlockSpec((rows, HEAD), lambda j: (0, j)),
        pl.BlockSpec((rows, HEAD), lambda j: (0, j + 4)),
    ]


QUERY_QUAD = pl.BlockSpec((2 * BLOCK, 4 * HEAD), lambda j: (0, j))
QUERY_PAIR = pl.BlockSpec((2 * BLOCK, 2 * HEAD), lambda j: (0, j))
SUMS = pl.BlockSpec((1, 2, 2 * BLOCK, 2 * HEAD), lambda j: (j, 0, 0, 0))


def near_attention(flags, queries, own, behind):
    return pl.pallas_call(
        near_kernel,
        out_shape=jax.ShapeDtypeStruct((4, 2, 2 * BLOCK, 2 * HEAD), F32),
        grid=(4,),
        in_specs=[SCALARS, QUERY_PAIR] + head_pair(512) + head_pair(512),
        out_specs=SUMS,
        compiler_params=params(16),
        cost_estimate=cost(8 * 512 * 768 * 512, 6 * MIB, 8 * 512 * 768),
    )(flags, queries, own, own, behind, behind)


def far_attention(flags, queries, sums, near, cross):
    return pl.pallas_call(
        far_kernel,
        out_shape=jax.ShapeDtypeStruct((2 * BLOCK, 1024), BF),
        grid=(2,),
        in_specs=[
            SCALARS,
            QUERY_QUAD,
            pl.BlockSpec((2, 2, 2 * BLOCK, 2 * HEAD), lambda j: (j, 0, 0, 0)),
        ]
        + [
            pl.BlockSpec((rows, 2 * HEAD), lambda j, shift=shift: (0, j + shift))
            for rows in (512, 256)
            for shift in (0, 2)
        ],
        out_specs=QUERY_QUAD,
        compiler_params=params(16),
        cost_estimate=cost(8 * 512 * 512 * 512, 6 * MIB, 8 * 512 * 512),
    )(flags, queries, sums, near, near, cross, cross)


OUT_TILE = 1792


def out_kernel(att_ref, weight_ref, out_ref):
    dims = (((1,), (1,)), ((), ()))
    at = pl.multiple_of(pl.program_id(0) * OUT_TILE, 128)
    got = lax.dot_general(
        att_ref[:, :512], weight_ref[pl.ds(at, OUT_TILE), :], dims, preferred_element_type=F32
    )
    got += lax.dot_general(
        att_ref[:, 512:], weight_ref[pl.ds(at + WIDTH, OUT_TILE), :], dims,
        preferred_element_type=F32,
    )
    out_ref[...] = got.astype(out_ref.dtype)


def out_projection(attended, weights, which, kind):
    return pl.pallas_call(
        out_kernel,
        out_shape=jax.ShapeDtypeStruct((BLOCK, WIDTH), kind),
        grid=(WIDTH // OUT_TILE,),
        in_specs=[
            pl.BlockSpec((BLOCK, 1024), lambda i: (which, 0)),
            pl.BlockSpec(memory_space=pltpu.VMEM),
        ],
        out_specs=pl.BlockSpec((BLOCK, OUT_TILE), lambda i: (0, i)),
        compiler_params=params(24),
        cost_estimate=cost(2 * BLOCK * 1024 * WIDTH, 15 * MIB),
    )(attended, weights)


def end_kernel(tok_ref, own_ref, got_ref, gain_ref, out_ref):
    whole = own_ref[...] + got_ref[...].astype(F32)
    mean_square = jnp.mean(whole * whole, axis=-1, keepdims=True)
    scaled = whole * lax.rsqrt(mean_square + epsilon) * gain_ref[...]
    out_ref[...] = (tok_ref[...].astype(F32) + scaled).astype(BF)


def ending(tokens, own, got, gain):
    rows = 128
    wide = pl.BlockSpec((rows, WIDTH), lambda i: (i, 0))
    return pl.pallas_call(
        end_kernel,
        out_shape=jax.ShapeDtypeStruct((BLOCK, WIDTH), BF),
        grid=(BLOCK // rows,),
        in_specs=[wide, wide, wide, pl.BlockSpec((1, WIDTH), lambda i: (0, 0))],
        out_specs=wide,
        compiler_params=params(24),
        cost_estimate=cost(10 * BLOCK * WIDTH, 14 * MIB),
    )(tokens, own, got, gain)


def rotations(positions):
    exponents = jnp.arange(HALF, dtype=F32) * (2.0 / HEAD)
    frequency = jnp.exp(-exponents * jnp.log(jnp.float32(rope_base)))
    angles = positions.astype(F32)[:, None] * frequency[None, :]
    cosine, sine = jnp.cos(angles), jnp.sin(angles)
    return (
        jnp.concatenate([cosine, cosine], axis=1),
        jnp.concatenate([-sine, sine], axis=1),
    )


def pack_kernel(core_ref, q_ref, k_ref, v_ref, o_ref, keep_ref, send_ref):
    def pack(to_ref, side):
        at = 0
        for ref in (q_ref, k_ref, v_ref, o_ref):
            width = ref.shape[1] // 2
            to_ref[:, at : at + width] = ref[:, side * width : (side + 1) * width]
            at += width

    for core in range(2):

        @pl.when(core_ref[0] == core)
        def _():
            pack(keep_ref, core)
            pack(send_ref, 1 - core)


def chip_weights(core, q, k, v, o):
    rows = q.shape[0]
    whole = pl.BlockSpec(memory_space=pltpu.VMEM)
    keep, send = pl.pallas_call(
        pack_kernel,
        out_shape=(jax.ShapeDtypeStruct((rows, 1536), BF),) * 2,
        in_specs=[SCALARS, whole, whole, whole, whole],
        out_specs=(whole, whole),
        compiler_params=params(60),
        cost_estimate=cost(0, 1 * MIB),
    )(core.astype(jnp.int32).reshape(1), q, k, v, o)
    got = lax.ppermute(send, "core", [(0, 1), (1, 0)])
    first, second = jnp.where(core == 0, keep, got), jnp.where(core == 0, got, keep)
    return jnp.concatenate([first, second], axis=0)


def on_device(
    tokens,
    norm_gain,
    query_weight,
    key_matrix,
    value_matrix,
    out_weight,
    query_gain,
    key_gain,
    post_gain,
):
    core = lax.axis_index("core")
    side = lax.axis_index("x_hi")
    chip = lax.axis_index(CHIPS)
    full = lax.all_gather(
        chip_weights(core, query_weight, key_matrix, value_matrix, out_weight),
        GATHER,
        axis=0,
        tiled=True,
    )

    plain = tokens.astype(F32)
    mean_square = jnp.mean(plain * plain, axis=-1, keepdims=True)
    normed = (plain * lax.rsqrt(mean_square + epsilon) * norm_gain).astype(BF)
    other = lax.ppermute(normed, "core", [(0, 1), (1, 0)])
    x = chip_rows(core, normed, other)
    row = jnp.arange(2 * BLOCK, dtype=jnp.int32)
    positions = (4 * chip + side) * BLOCK + row + (row // BLOCK) * BLOCK
    cosine, sine = rotations(positions)


    own = key_values(x, full, key_gain.reshape(1, HEAD), cosine, sine)
    line = CHIPS + ("x_hi",)
    chips = 32
    single = jnp.where(side == 0, own[BLOCK:], own[:BLOCK])
    near = lax.ppermute(own, line, [(i, i + 1) for i in range(2 * chips - 1)])
    behind = lax.ppermute(own, CHIPS, [(i, i + 1) for i in range(chips - 1)])
    cross = lax.ppermute(
        single, line,
        [(2 * i + 1, 2 * i) for i in range(chips)]
        + [(2 * i, 2 * i + 3) for i in range(chips - 1)],
    )
    queries = projection(
        query_kernel, x, full, query_gain.reshape(1, HEAD), cosine, sine,
        lambda t: (t // 2, lax.rem(t, 2)),
    )
    later = (chip > 0).astype(jnp.int32)
    flags = jnp.stack([later, jnp.maximum(later, side), core, side]).astype(jnp.int32)
    sums = near_attention(flags, queries, own, behind)
    out_rows, _ = lax.optimization_barrier((full, own))
    out_rows = out_rows[:, 1024:]
    attended = far_attention(flags, queries, sums, near, cross)
    theirs = out_projection(attended, out_rows, 1, BF)
    got = lax.ppermute(theirs, "core", [(0, 1), (1, 0)])
    ours = out_projection(attended, out_rows, 0, F32)
    return ending(tokens, ours, got, post_gain.reshape(1, WIDTH))


def solution(mesh):
    spread = Mesh(mesh.devices.reshape(2, 4, 4, 2, 2), AXES)
    whole = P(AXES, None)
    rows = P(AXES[:4], "x_hi")
    return jax.shard_map(
        on_device,
        mesh=spread,
        in_specs=(whole, P(), rows, rows, rows, rows, P(), P(), P()),
        out_specs=whole,
        check_vma=False,
    )
```

```python
import math

import jax
import jax.numpy as jnp
from jax import lax
from jax.experimental import pallas as pl
from jax.experimental.pallas import tpu as pltpu
from jax.sharding import Mesh, PartitionSpec as P

HEAD = 128
HALF = HEAD // 2
BLOCK = 256
WIDTH = 5376
AXES = ("x_lo", "y", "z", "core", "x_hi")
CHIPS = ("x_lo", "y", "z")
GATHER = ("x_hi", "x_lo", "y", "z")
epsilon = 1e-06
query_scale = 168.0 ** (-0.5) * math.log2(math.e)
rope_base = 10000.0
BF = jnp.bfloat16
F32 = jnp.float32
MIB = 1 << 20
SCALARS = pl.BlockSpec(memory_space=pltpu.SMEM)


def cost(flops, size, exps=0):
    return pl.CostEstimate(flops=int(flops), bytes_accessed=int(size), transcendentals=int(exps))


def params(mib):
    return pltpu.CompilerParams(vmem_limit_bytes=mib * MIB)


def turned(raw, gain, cosine, sine, scale):
    mean_square = jnp.mean(raw * raw, axis=-1, keepdims=True)
    unit = raw * (lax.rsqrt(mean_square + epsilon) * scale) * gain
    return unit * cosine + pltpu.roll(unit, HALF, axis=1) * sine


def key_value_kernel(x_ref, low_ref, high_ref, gain_ref, cos_ref, sin_ref, out_ref, sum_ref):
    step = pl.program_id(0)
    terms = [
        jnp.dot(x_ref[...], ref[...], preferred_element_type=F32) for ref in (low_ref, high_ref)
    ]

    @pl.when(step == 0)
    def _():
        for n in range(2):
            sum_ref[n] = terms[n]

    @pl.when(step > 0)
    def _():
        for n in range(2):
            sum_ref[n] += terms[n]

    @pl.when(step == pl.num_programs(0) - 1)
    def _():
        for n in range(2):
            for h in range(2):
                raw = sum_ref[n, :, h * HEAD : (h + 1) * HEAD]
                key = turned(raw, gain_ref[...], cos_ref[...], sin_ref[...], 1.0)
                out_ref[:, (2 * n + h) * HEAD : (2 * n + h + 1) * HEAD] = key.astype(BF)
            out_ref[:, 512 + 256 * n : 768 + 256 * n] = sum_ref[n, :, 256:].astype(BF)


def key_values(x, weights, gain, cosine, sine):
    rows, steps = x.shape[0], 3
    depth = WIDTH // steps

    def whole(shape):
        return pl.BlockSpec(shape, lambda t: (0, 0))

    return pl.pallas_call(
        key_value_kernel,
        out_shape=jax.ShapeDtypeStruct((rows, 1024), BF),
        grid=(steps,),
        in_specs=[
            pl.BlockSpec((rows, depth), lambda t: (0, t)),
            pl.BlockSpec((depth, 512), lambda t: (t, 1)),
            pl.BlockSpec((depth, 512), lambda t: (t + steps, 1)),
            whole((1, HEAD)),
            whole((rows, HEAD)),
            whole((rows, HEAD)),
        ],
        out_specs=whole((rows, 1024)),
        scratch_shapes=[pltpu.VMEM((2, rows, 512), F32)],
        compiler_params=params(60),
        cost_estimate=cost(2 * rows * WIDTH * 1024, 2 * WIDTH * 1536),
    )(x, weights, weights, gain, cosine, sine)


def query_kernel(x_ref, w_ref, gain_ref, cos_ref, sin_ref, out_ref):
    raw = jnp.dot(x_ref[...], w_ref[...], preferred_element_type=F32)
    for h in range(2):
        at = slice(h * HEAD, (h + 1) * HEAD)
        query = turned(raw[:, at], gain_ref[...], cos_ref[...], sin_ref[...], query_scale)
        out_ref[:, at] = query.astype(BF)


def chip_rows_kernel(core_ref, mine_ref, other_ref, out_ref):
    core = core_ref[0]
    for ref, which in ((mine_ref, core), (other_ref, 1 - core)):
        out_ref[pl.ds(pl.multiple_of(which * BLOCK, BLOCK), BLOCK), :] = ref[...]


def chip_rows(core, mine, other):
    whole = pl.BlockSpec(memory_space=pltpu.VMEM)
    return pl.pallas_call(
        chip_rows_kernel,
        out_shape=jax.ShapeDtypeStruct((2 * BLOCK, WIDTH), BF),
        in_specs=[SCALARS, whole, whole],
        out_specs=whole,
        compiler_params=params(16),
        cost_estimate=cost(0, 12 * MIB),
    )(core.astype(jnp.int32).reshape(1), mine, other)


def projection(kernel, x, weights, gain, cosine, sine, where):
    rows = x.shape[0]
    whole = pl.BlockSpec(memory_space=pltpu.VMEM)
    return pl.pallas_call(
        kernel,
        out_shape=jax.ShapeDtypeStruct((rows, 1024), BF),
        grid=(4,),
        in_specs=[whole, pl.BlockSpec((WIDTH, 256), where), whole, whole, whole],
        out_specs=pl.BlockSpec((rows, 256), lambda t: (0, t)),
        compiler_params=params(20),
        cost_estimate=cost(2 * rows * WIDTH * 1024, 2 * WIDTH * 1536),
    )(x, weights, gain, cosine, sine)


def attend(query, keys, total):
    row = lax.rem(lax.broadcasted_iota(jnp.int32, (2 * BLOCK, BLOCK), 0), BLOCK)
    col = lax.broadcasted_iota(jnp.int32, (2 * BLOCK, BLOCK), 1)
    for key, value, count, edge in keys:
        score = lax.dot_general(query, key, (((1,), (1,)), ((), ())), preferred_element_type=F32)
        raised = jnp.exp2(score)
        if edge == "oldest":
            raised = jnp.where(col > row, raised, 0.0)
        if edge == "own":
            raised = jnp.where(col <= row, raised, 0.0)
        counted = jnp.concatenate([value, count], axis=1)
        total += jnp.dot(raised.astype(BF), counted, preferred_element_type=F32)
    return total


def counts(flag):
    lane = lax.broadcasted_iota(jnp.int32, (BLOCK, HEAD), 1)
    return jnp.where(lane == 0, flag.astype(F32), 0.0).astype(BF)


def both_heads(q_ref, part):
    at = slice(part * BLOCK, (part + 1) * BLOCK)
    return jnp.concatenate([q_ref[at, :HEAD], q_ref[at, HEAD:]], axis=0)


def near_kernel(flag_ref, q_ref, ok, ov, zk, zv, sum_ref):
    early, always = counts(flag_ref[0]), counts(jnp.int32(1))
    first, second = slice(0, BLOCK), slice(BLOCK, 2 * BLOCK)
    keys = (
        (
            (zk[first], zv[first], early, "oldest"),
            (zk[second], zv[second], early, ""),
            (ok[first], ov[first], always, "own"),
        ),
        (
            (zk[second], zv[second], early, "oldest"),
            (ok[first], ov[first], always, ""),
            (ok[second], ov[second], always, "own"),
        ),
    )
    for part in range(2):
        start = jnp.zeros((2 * BLOCK, 2 * HEAD), F32)
        sum_ref[0, part] = attend(both_heads(q_ref, part), keys[part], start)


def far_kernel(flag_ref, q_ref, sum_ref, nk, nv, ck, cv, out_ref):
    core, side = flag_ref[2], flag_ref[3]
    early, late, always = counts(flag_ref[0]), counts(flag_ref[1]), counts(jnp.int32(1))
    before = pl.ds(pl.multiple_of((1 - side) * BLOCK, BLOCK), BLOCK)
    beside = pl.ds(pl.multiple_of(side * BLOCK, BLOCK), BLOCK)
    for head in range(2):
        lanes = slice(head * HEAD, (head + 1) * HEAD)
        wide = slice(head * 2 * HEAD, (head + 1) * 2 * HEAD)
        gap = tuple(
            jnp.where(side == 0, n[beside, lanes], c[:, lanes]) for n, c in ((nk, ck), (nv, cv))
        )
        link = tuple(
            jnp.where(side == 0, c[:, lanes], n[beside, lanes]) for n, c in ((nk, ck), (nv, cv))
        )
        gap, link = gap + (early, ""), link + (always, "")
        prior = (nk[before, lanes], nv[before, lanes], late, "")
        for part, keys in enumerate(((gap, prior), (prior, link))):
            query = both_heads(q_ref.at[:, wide], part)
            total = attend(query, keys, sum_ref[head, part])
            mixed = (total[:, :HEAD] / total[:, HEAD : HEAD + 1]).astype(BF)
            to = pl.ds(pl.multiple_of(lax.rem(part + core, 2) * BLOCK, BLOCK), BLOCK)
            out_ref[to, wide] = jnp.concatenate([mixed[:BLOCK], mixed[BLOCK:]], axis=1)


def head_pair(rows):
    return [
        pl.BlockSpec((rows, HEAD), lambda j: (0, j)),
        pl.BlockSpec((rows, HEAD), lambda j: (0, j + 4)),
    ]


QUERY_QUAD = pl.BlockSpec((2 * BLOCK, 4 * HEAD), lambda j: (0, j))
QUERY_PAIR = pl.BlockSpec((2 * BLOCK, 2 * HEAD), lambda j: (0, j))
SUMS = pl.BlockSpec((1, 2, 2 * BLOCK, 2 * HEAD), lambda j: (j, 0, 0, 0))


def near_attention(flags, queries, own, behind):
    return pl.pallas_call(
        near_kernel,
        out_shape=jax.ShapeDtypeStruct((4, 2, 2 * BLOCK, 2 * HEAD), F32),
        grid=(4,),
        in_specs=[SCALARS, QUERY_PAIR] + head_pair(512) + head_pair(512),
        out_specs=SUMS,
        compiler_params=params(16),
        cost_estimate=cost(8 * 512 * 768 * 512, 6 * MIB, 8 * 512 * 768),
    )(flags, queries, own, own, behind, behind)


def far_attention(flags, queries, sums, near, cross):
    return pl.pallas_call(
        far_kernel,
        out_shape=jax.ShapeDtypeStruct((2 * BLOCK, 1024), BF),
        grid=(2,),
        in_specs=[
            SCALARS,
            QUERY_QUAD,
            pl.BlockSpec((2, 2, 2 * BLOCK, 2 * HEAD), lambda j: (j, 0, 0, 0)),
        ]
        + [
            pl.BlockSpec((rows, 2 * HEAD), lambda j, shift=shift: (0, j + shift))
            for rows in (512, 256)
            for shift in (0, 2)
        ],
        out_specs=QUERY_QUAD,
        compiler_params=params(16),
        cost_estimate=cost(8 * 512 * 512 * 512, 6 * MIB, 8 * 512 * 512),
    )(flags, queries, sums, near, near, cross, cross)


OUT_TILE = 2688


def out_kernel(att_ref, weight_ref, out_ref):
    dims = (((1,), (1,)), ((), ()))
    at = pl.multiple_of(pl.program_id(0) * OUT_TILE, 128)
    got = lax.dot_general(
        att_ref[:, :512], weight_ref[pl.ds(at, OUT_TILE), :], dims, preferred_element_type=F32
    )
    got += lax.dot_general(
        att_ref[:, 512:], weight_ref[pl.ds(at + WIDTH, OUT_TILE), :], dims,
        preferred_element_type=F32,
    )
    out_ref[...] = got.astype(out_ref.dtype)


def out_projection(attended, weights, which, kind):
    return pl.pallas_call(
        out_kernel,
        out_shape=jax.ShapeDtypeStruct((BLOCK, WIDTH), kind),
        grid=(WIDTH // OUT_TILE,),
        in_specs=[
            pl.BlockSpec((BLOCK, 1024), lambda i: (which, 0)),
            pl.BlockSpec(memory_space=pltpu.VMEM),
        ],
        out_specs=pl.BlockSpec((BLOCK, OUT_TILE), lambda i: (0, i)),
        compiler_params=params(24),
        cost_estimate=cost(2 * BLOCK * 1024 * WIDTH, 15 * MIB),
    )(attended, weights)


def end_kernel(tok_ref, own_ref, got_ref, gain_ref, out_ref):
    whole = own_ref[...] + got_ref[...].astype(F32)
    mean_square = jnp.mean(whole * whole, axis=-1, keepdims=True)
    scaled = whole * lax.rsqrt(mean_square + epsilon) * gain_ref[...]
    out_ref[...] = (tok_ref[...].astype(F32) + scaled).astype(BF)


def ending(tokens, own, got, gain):
    rows = 128
    wide = pl.BlockSpec((rows, WIDTH), lambda i: (i, 0))
    return pl.pallas_call(
        end_kernel,
        out_shape=jax.ShapeDtypeStruct((BLOCK, WIDTH), BF),
        grid=(BLOCK // rows,),
        in_specs=[wide, wide, wide, pl.BlockSpec((1, WIDTH), lambda i: (0, 0))],
        out_specs=wide,
        compiler_params=params(24),
        cost_estimate=cost(10 * BLOCK * WIDTH, 14 * MIB),
    )(tokens, own, got, gain)


def rotations(positions):
    exponents = jnp.arange(HALF, dtype=F32) * (2.0 / HEAD)
    frequency = jnp.exp(-exponents * jnp.log(jnp.float32(rope_base)))
    angles = positions.astype(F32)[:, None] * frequency[None, :]
    cosine, sine = jnp.cos(angles), jnp.sin(angles)
    return (
        jnp.concatenate([cosine, cosine], axis=1),
        jnp.concatenate([-sine, sine], axis=1),
    )


def pack_kernel(core_ref, q_ref, k_ref, v_ref, o_ref, keep_ref, send_ref):
    def pack(to_ref, side):
        at = 0
        for ref in (q_ref, k_ref, v_ref, o_ref):
            width = ref.shape[1] // 2
            to_ref[:, at : at + width] = ref[:, side * width : (side + 1) * width]
            at += width

    for core in range(2):

        @pl.when(core_ref[0] == core)
        def _():
            pack(keep_ref, core)
            pack(send_ref, 1 - core)


def chip_weights(core, q, k, v, o):
    rows = q.shape[0]
    whole = pl.BlockSpec(memory_space=pltpu.VMEM)
    keep, send = pl.pallas_call(
        pack_kernel,
        out_shape=(jax.ShapeDtypeStruct((rows, 1536), BF),) * 2,
        in_specs=[SCALARS, whole, whole, whole, whole],
        out_specs=(whole, whole),
        compiler_params=params(60),
        cost_estimate=cost(0, 1 * MIB),
    )(core.astype(jnp.int32).reshape(1), q, k, v, o)
    got = lax.ppermute(send, "core", [(0, 1), (1, 0)])
    first, second = jnp.where(core == 0, keep, got), jnp.where(core == 0, got, keep)
    return jnp.concatenate([first, second], axis=0)


def on_device(
    tokens,
    norm_gain,
    query_weight,
    key_matrix,
    value_matrix,
    out_weight,
    query_gain,
    key_gain,
    post_gain,
):
    core = lax.axis_index("core")
    side = lax.axis_index("x_hi")
    chip = lax.axis_index(CHIPS)
    full = lax.all_gather(
        chip_weights(core, query_weight, key_matrix, value_matrix, out_weight),
        GATHER,
        axis=0,
        tiled=True,
    )

    plain = tokens.astype(F32)
    mean_square = jnp.mean(plain * plain, axis=-1, keepdims=True)
    normed = (plain * lax.rsqrt(mean_square + epsilon) * norm_gain).astype(BF)
    other = lax.ppermute(normed, "core", [(0, 1), (1, 0)])
    x = chip_rows(core, normed, other)
    row = jnp.arange(2 * BLOCK, dtype=jnp.int32)
    positions = (4 * chip + side) * BLOCK + row + (row // BLOCK) * BLOCK
    cosine, sine = rotations(positions)


    own = key_values(x, full, key_gain.reshape(1, HEAD), cosine, sine)
    line = CHIPS + ("x_hi",)
    chips = 32
    single = jnp.where(side == 0, own[BLOCK:], own[:BLOCK])
    near = lax.ppermute(own, line, [(i, i + 1) for i in range(2 * chips - 1)])
    behind = lax.ppermute(own, CHIPS, [(i, i + 1) for i in range(chips - 1)])
    cross = lax.ppermute(
        single, line,
        [(2 * i + 1, 2 * i) for i in range(chips)]
        + [(2 * i, 2 * i + 3) for i in range(chips - 1)],
    )
    queries = projection(
        query_kernel, x, full, query_gain.reshape(1, HEAD), cosine, sine,
        lambda t: (t // 2, lax.rem(t, 2)),
    )
    later = (chip > 0).astype(jnp.int32)
    flags = jnp.stack([later, jnp.maximum(later, side), core, side]).astype(jnp.int32)
    sums = near_attention(flags, queries, own, behind)
    out_rows, _ = lax.optimization_barrier((full, own))
    out_rows = out_rows[:, 1024:]
    attended = far_attention(flags, queries, sums, near, cross)
    theirs = out_projection(attended, out_rows, 1, BF)
    got = lax.ppermute(theirs, "core", [(0, 1), (1, 0)])
    ours = out_projection(attended, out_rows, 0, F32)
    return ending(tokens, ours, got, post_gain.reshape(1, WIDTH))


def solution(mesh):
    spread = Mesh(mesh.devices.reshape(2, 4, 4, 2, 2), AXES)
    whole = P(AXES, None)
    rows = P(AXES[:4], "x_hi")
    return jax.shard_map(
        on_device,
        mesh=spread,
        in_specs=(whole, P(), rows, rows, rows, rows, P(), P(), P()),
        out_specs=whole,
        check_vma=False,
    )
```
